256 devices in a mesh: user: 16 (over z, core), item: 16 (over y, x).
Axes of the slice: x: 4, y: 4, z: 8, core: 2. Of those that a mesh axis runs over, the one named last changes fastest.
Arguments:
- user_factors: float32 [8192, 256], P('user'), may hold values from -0.3 to 0.3, as said below
- item_factors: float32 [8192, 256], P('item'), may hold values from -0.6 to 0.6
- tile_user: int32 [16, 16, 16, 2], P('item', 'user'), may hold values from 0 to 3
- tile_item: int32 [16, 16, 16, 2], P('item', 'user'), may hold values from 0 to 3
- tile_count: int32 [16, 16, 16], P('item', 'user'), may hold values from 1 to 2, as said below
- tile_conf: bfloat16 [16, 16, 16, 2, 128, 128], P('item', 'user'), may hold values from 0.099609375 to 4
- held_user: int32 [16, 16, 16, 2], P('user', 'item'), may hold values from 0 to 1
- held_item: int32 [16, 16, 16, 2], P('user', 'item'), may hold values from 0 to 3
- held_count: int32 [16, 16, 16], P('user', 'item'), may hold values from 1 to 2, as said below
- held_conf: bfloat16 [16, 16, 16, 2, 128, 128], P('user', 'item'), may hold values from 0.099609375 to 4
Outputs:
- new_items: float32 [8192, 256], P('item')
- folded_users: float32 [4096, 256], P('user')
The draws below stay inside these ranges and needn't reach their ends.
Inputs may be any that keep to these rules, and one draw needn't show every extreme that they name: `user_factors`: user factors; the scale of a factor column varies by up to a factor of ten. `tile_count`: some device has an owner with all 2 slots live and one with a single live slot. `held_count`: some device has an owner with all 2 slots live and one with a single live slot.
All inputs are finite; a program needn't handle non-finite values.
Results may differ from the reference program's by a relative error of at most 0.0003.
Values may be sent and summed in bfloat16 or wider, within the bound.
No kernel may reach another device: no remote copies, remote signals or barrier semaphores. Data moves between devices by JAX's collectives and lax.ppermute only.
A program may use at most 128 MiB of HBM per device.

```python
import math
import jax
import jax.numpy as jnp
from jax import lax

K = 256
BL = 128
UB_DEV = 4
IB_DEV = 4
HB_DEV = 2
CAP = 2
HCAP = 2
ITERS = 2
USERS = 8192
ITEMS = 8192
HELD = 4096
N_USER = 16
N_ITEM = 16


def draw_user_factors(key, part):
    scale_key, value_key = jax.random.split(jax.random.fold_in(key, 7))
    scales = jnp.exp(jax.random.uniform(scale_key, (K,), jnp.float32, 0.0, math.log(10.0)))
    values = jax.random.uniform(value_key, (USERS, K), jnp.float32, -1.0, 1.0)
    return values * scales[None, :] * 0.03


def draw_tile_count(key, part):
    counts = jax.random.randint(jax.random.fold_in(key, 3), (N_ITEM, N_USER, N_USER), 1, CAP + 1)
    counts = counts.at[0, 0, 0].set(CAP)
    return counts.at[0, 0, 1].set(1)


def draw_held_count(key, part):
    counts = jax.random.randint(jax.random.fold_in(key, 5), (N_USER, N_ITEM, N_ITEM), 1, HCAP + 1)
    counts = counts.at[0, 0, 0].set(HCAP)
    return counts.at[0, 0, 1].set(1)


def set_ends(array, stream_key, smallest, high):
    longest = array.shape.index(max(array.shape))
    spots = []
    for shift in (0, 1):
        where = [jax.random.randint(jax.random.fold_in(stream_key, axis), (), 0, length) for axis, length in enumerate(array.shape)]
        where[longest] = (where[longest] + shift) % array.shape[longest]
        spots.append(tuple(where))
    return array.at[spots[0]].set(smallest).at[spots[1]].set(high)


def steps_of(own_key, extent, shards, least, top_value):
    loudness = 1.0
    for dim, blocks in shards:
        steps = jax.random.uniform(jax.random.fold_in(jax.random.fold_in(own_key, 6), dim), (blocks,), jnp.float32, least / len(shards), top_value / len(shards))
        loudness = loudness * jnp.repeat(jnp.exp(steps), extent[dim] // blocks).reshape((-1,) + (1,) * (len(extent) - 1 - dim))
    return loudness


def noise(rng, extent, spread, limit, cuts=(), kind=jnp.bfloat16):
    loudness = steps_of(rng, extent, cuts, -0.22, 0.18) if cuts else 1.0
    array = jax.random.normal(rng, extent, jnp.float32) * spread * loudness
    return jnp.minimum(jnp.maximum(array, -limit), limit).astype(kind)


def setup_inputs(seed: int = 0) -> dict:
    streams_of = jax.random.split(jax.random.key(seed), 11)
    user_factors = draw_user_factors(jax.random.fold_in(streams_of[10], 71), 0)
    item_factors = noise(streams_of[1], (ITEMS, K), 0.1, 0.6, ((0, 16),), jnp.float32)
    tile_user = set_ends(jax.random.randint(streams_of[2], (N_ITEM, N_USER, N_USER, CAP), 0, UB_DEV), jax.random.fold_in(streams_of[2], 1), 0, UB_DEV - 1).astype(jnp.int32)
    tile_item = set_ends(jax.random.randint(streams_of[3], (N_ITEM, N_USER, N_USER, CAP), 0, IB_DEV), jax.random.fold_in(streams_of[3], 1), 0, IB_DEV - 1).astype(jnp.int32)
    tile_count = draw_tile_count(jax.random.fold_in(streams_of[10], 71), 0)
    tile_conf = jnp.clip(jnp.exp(math.log(4.0) - 3.6927934 * jax.random.uniform(streams_of[5], (N_ITEM, N_USER, N_USER, CAP, BL, BL), jnp.float32) ** steps_of(streams_of[5], (N_ITEM, N_USER, N_USER, CAP, BL, BL), ((0, 16), (1, 16)), -0.2, 0.2)), 0.099609375, 4.0).astype(jnp.bfloat16)
    held_user = set_ends(jax.random.randint(streams_of[6], (N_USER, N_ITEM, N_ITEM, HCAP), 0, HB_DEV), jax.random.fold_in(streams_of[6], 1), 0, HB_DEV - 1).astype(jnp.int32)
    held_item = set_ends(jax.random.randint(streams_of[7], (N_USER, N_ITEM, N_ITEM, HCAP), 0, IB_DEV), jax.random.fold_in(streams_of[7], 1), 0, IB_DEV - 1).astype(jnp.int32)
    held_count = draw_held_count(jax.random.fold_in(streams_of[10], 71), 0)
    held_conf = jnp.clip(jnp.exp(math.log(4.0) - 3.6927934 * jax.random.uniform(streams_of[9], (N_USER, N_ITEM, N_ITEM, HCAP, BL, BL), jnp.float32) ** steps_of(streams_of[9], (N_USER, N_ITEM, N_ITEM, HCAP, BL, BL), ((0, 16), (1, 16)), -0.2, 0.2)), 0.099609375, 4.0).astype(jnp.bfloat16)
    return dict(user_factors=user_factors, item_factors=item_factors, tile_user=tile_user, tile_item=tile_item, tile_count=tile_count, tile_conf=tile_conf, held_user=held_user, held_item=held_item, held_count=held_count, held_conf=held_conf)


highest = lax.Precision.HIGHEST
ridge_weight = 1.0
epsilon = 1e-6


def local_gram(rows):
    return jnp.einsum('nk,nm->km', rows, rows, precision=highest)


def gram_apply(vector, gram):
    return jnp.einsum('jck,km->jcm', vector, gram, precision=highest) + ridge_weight * vector


def block_onehot(positions, blocks):
    return (positions[:, None] == jnp.arange(blocks, dtype=jnp.int32)[None, :]).astype(jnp.float32)


def item_terms(factors, weights, positions, onehot, vector):
    picked = vector[positions]
    scores = jnp.einsum('tuk,tik->tui', factors, picked, precision=highest) * weights
    terms = jnp.einsum('tui,tuk->tik', scores, factors, precision=highest)
    return jnp.einsum('tj,tik->jik', onehot, terms, precision=highest)


def item_right(factors, right_weights, onehot):
    terms = jnp.einsum('tui,tuk->tik', right_weights, factors, precision=highest)
    return jnp.einsum('tj,tik->jik', onehot, terms, precision=highest)


def held_terms(factors, weights, positions, onehot, vector):
    picked = vector[positions]
    scores = jnp.einsum('tik,thk->thi', factors, picked, precision=highest) * weights
    terms = jnp.einsum('thi,tik->thk', scores, factors, precision=highest)
    return jnp.einsum('tj,thk->jhk', onehot, terms, precision=highest)


def held_right(factors, right_weights, onehot):
    terms = jnp.einsum('thi,tik->thk', right_weights, factors, precision=highest)
    return jnp.einsum('tj,thk->jhk', onehot, terms, precision=highest)


def conjugate(operator, residual, start):
    solution = start
    direction = residual
    norm_now = jnp.sum(residual * residual, axis=-1, keepdims=True)
    for iteration in range(ITERS):
        image = operator(direction)
        alpha = norm_now / (jnp.sum(direction * image, axis=-1, keepdims=True) + epsilon)
        solution = solution + alpha * direction
        residual = residual - alpha * image
        norm_next = jnp.sum(residual * residual, axis=-1, keepdims=True)
        direction = residual + (norm_next / (norm_now + epsilon)) * direction
        norm_now = norm_next
    return solution


def reference(user_factors, item_factors, tile_user, tile_item, tile_count, tile_conf, held_user, held_item, held_count, held_conf):
    gram_users = local_gram(user_factors)
    user_blocks = user_factors.reshape(N_USER * UB_DEV, BL, K)
    user_owner = jnp.arange(N_USER, dtype=jnp.int32)[:, None] * UB_DEV

    def item_shard(packed):
        user_index, item_index, tile_counts, confidence, warm_start = packed
        named_blocks = (user_owner + user_index).reshape(-1)
        factors = user_blocks[named_blocks]
        live_flat = (jnp.arange(CAP, dtype=jnp.int32)[None, None, :] < tile_counts[:, :, None]).astype(jnp.float32).reshape(-1)[:, None, None]
        conf_flat = confidence.reshape(-1, BL, BL).astype(jnp.float32)
        weights = conf_flat * live_flat
        right_weights = (1.0 + conf_flat) * live_flat
        positions = item_index.reshape(-1)
        onehot = block_onehot(positions, IB_DEV)
        start_blocks = warm_start.reshape(IB_DEV, BL, K)

        def operator(direction):
            return item_terms(factors, weights, positions, onehot, direction) + gram_apply(direction, gram_users)

        residual = item_right(factors, right_weights, onehot) - operator(start_blocks)
        return conjugate(operator, residual, start_blocks).reshape(IB_DEV * BL, K)

    new_items = lax.map(item_shard, (tile_user, tile_item, tile_count, tile_conf, item_factors.reshape(N_ITEM, IB_DEV * BL, K))).reshape(ITEMS, K)

    gram_items = local_gram(new_items)
    item_blocks = new_items.reshape(N_ITEM * IB_DEV, BL, K)
    item_owner = jnp.arange(N_ITEM, dtype=jnp.int32)[:, None] * IB_DEV

    def held_shard(packed):
        held_index, owner_index, held_counts, confidence = packed
        named_blocks = (item_owner + owner_index).reshape(-1)
        factors = item_blocks[named_blocks]
        live_flat = (jnp.arange(HCAP, dtype=jnp.int32)[None, None, :] < held_counts[:, :, None]).astype(jnp.float32).reshape(-1)[:, None, None]
        conf_flat = confidence.reshape(-1, BL, BL).astype(jnp.float32)
        weights = conf_flat * live_flat
        right_weights = (1.0 + conf_flat) * live_flat
        positions = held_index.reshape(-1)
        onehot = block_onehot(positions, HB_DEV)

        def operator(direction):
            return held_terms(factors, weights, positions, onehot, direction) + gram_apply(direction, gram_items)

        residual = held_right(factors, right_weights, onehot)
        zero_start = jnp.zeros((HB_DEV, BL, K), jnp.float32)
        return conjugate(operator, residual, zero_start).reshape(HB_DEV * BL, K)

    folded_users = lax.map(held_shard, (held_user, held_item, held_count, held_conf)).reshape(HELD, K)
    return new_items, folded_users
```

```python
import functools

import jax
import jax.numpy as jnp
from jax import lax
from jax.experimental import pallas as pl
from jax.experimental.pallas import tpu as pltpu
from jax.sharding import PartitionSpec as P

ITERS = 2
LAM = 1.0
EPS = 1e-6
BL = 128
SUB = 8
VMEM = 56 * 1024 * 1024

i32 = jnp.int32
f32 = jnp.float32
bf16 = jnp.bfloat16


def params():
    return pltpu.CompilerParams(vmem_limit_bytes=VMEM)


def vspec():
    return pl.BlockSpec(memory_space=pltpu.VMEM)


def power_of_two(exponent):
    bits = exponent + 126
    value = jnp.full(exponent.shape, 2.0**-126, f32)
    for k, power in enumerate((1, 2, 4, 8, 16, 32, 64)):
        value = value * jnp.where((bits >> k) & 1 == 1, f32(2.0**power), f32(1.0))
    high = jnp.where(bits >= 128, f32(2.0**64), f32(1.0))
    return value * high * high


def column_exponents(peak):
    rest = jnp.clip(peak, 2.0**-45, 2.0**60) * f32(2.0**60)
    found = jnp.zeros(peak.shape, i32)
    for k in (64, 32, 16, 8, 4, 2, 1):
        big = rest >= f32(2.0**k)
        rest = jnp.where(big, rest * f32(2.0**-k), rest)
        found = found + jnp.where(big, k, 0)
    return found - 74


def fixed_point(rows, inverse_step):
    return jnp.clip(jnp.round(rows * inverse_step), -32767.0, 32767.0).astype(i32)


def pack_users_kernel(rows_ref, out_ref):
    half = rows_ref.shape[0] // 2
    rows = rows_ref[...]
    exponent = column_exponents(jnp.max(jnp.abs(rows), axis=0, keepdims=True))
    inverse = power_of_two(-exponent)
    upper = fixed_point(rows_ref[:half, :], inverse)
    lower = fixed_point(rows_ref[half:, :], inverse)
    out_ref[:half, :] = (upper << 16) | (lower & 0xFFFF)
    out_ref[half:, :] = jnp.broadcast_to(exponent, (8, rows.shape[1]))


def pack_users(rows):
    half = rows.shape[0] // 2
    return pl.pallas_call(
        pack_users_kernel,
        out_shape=jax.ShapeDtypeStruct((half + 8, rows.shape[1]), i32),
        in_specs=[vspec()],
        out_specs=vspec(),
        name="pack_users",
    )(rows)


def pack_items_kernel(rows_ref, out_ref):
    peers, rows, rank = rows_ref.shape
    blocks = rows // SUB
    peak = jnp.max(jnp.max(jnp.abs(rows_ref[...]), axis=0), axis=0, keepdims=True)
    exponent = column_exponents(peak)
    inverse = power_of_two(-exponent)
    for b in range(blocks):
        for z in range(0, peers, 2):
            pair = jnp.concatenate(
                [rows_ref[z, b * SUB : (b + 1) * SUB, :], rows_ref[z + 1, b * SUB : (b + 1) * SUB, :]], axis=0
            )
            start = (b * peers + z) * SUB
            out_ref[start : start + 2 * SUB, :] = fixed_point(pair, inverse).astype(jnp.int16)
    out_ref[peers * rows :, :] = jnp.broadcast_to(exponent, (16, rank)).astype(jnp.int16)


def pack_items(rows):
    peers, count, rank = rows.shape
    return pl.pallas_call(
        pack_items_kernel,
        out_shape=jax.ShapeDtypeStruct((peers * count + 16, rank), jnp.int16),
        in_specs=[vspec()],
        out_specs=vspec(),
        name="pack_items",
    )(rows)


def dense_kernel(blocks, slots, codes_ref, strips_ref, ones_ref, right_ref, sums_ref, live_ref):
    sources = strips_ref.shape[0]
    sums_ref[...] = jnp.zeros_like(sums_ref)

    def clear(b, carry):
        live_ref[b] = 0
        return carry

    lax.fori_loop(0, blocks + 1, clear, 0)

    def add(s, carry):
        for pair in range(slots // 2):
            two = strips_ref[s, pair * 2 * SUB : (pair + 1) * 2 * SUB, :].astype(f32)
            for k in range(2):
                code = codes_ref[s * slots + pair * 2 + k]
                sums_ref[code] += two[k * SUB : (k + 1) * SUB, :]
                live_ref[code] = live_ref[code] + 1
        return carry

    lax.fori_loop(0, sources, add, 0)

    def finish(b, carry):
        total = sums_ref[b]
        ones_ref[b] = total + 1.0
        right_ref[b] = total + live_ref[b].astype(f32)
        return carry

    lax.fori_loop(0, blocks, finish, 0)


def dense(codes, strips, blocks, slots, name):
    shape = jax.ShapeDtypeStruct((blocks, SUB, BL), f32)
    return pl.pallas_call(
        functools.partial(dense_kernel, blocks, slots),
        out_shape=(shape, shape),
        in_specs=[pl.BlockSpec(memory_space=pltpu.SMEM), vspec()],
        out_specs=(vspec(), vspec()),
        scratch_shapes=[pltpu.VMEM((blocks + 1, SUB, BL), f32), pltpu.SMEM((blocks + 1,), i32)],
        compiler_params=params(),
        cost_estimate=pl.CostEstimate(flops=10**6, bytes_accessed=3 * 10**6, transcendentals=0),
        name=name,
    )(codes, strips)


NT = (((1,), (1,)), ((), ()))
NN = (((1,), (0,)), ((), ()))


def two_planes(value):
    upper = value.astype(bf16)
    return jnp.concatenate([upper, (value - upper.astype(f32)).astype(bf16)], axis=0)


def fold(both):
    rows = both.shape[0] // 2
    return both[:rows] + both[rows:]


def scores(direction, upper, lower):
    return fold(
        lax.dot_general(direction, upper, NT, preferred_element_type=f32)
        + lax.dot_general(direction, lower, NT, preferred_element_type=f32)
    )


def combine(weighted, upper, lower):
    planes = two_planes(weighted)
    return lax.dot_general(planes, upper, NN, preferred_element_type=f32) + lax.dot_general(
        planes, lower, NN, preferred_element_type=f32
    )


def pair_of(ref, t):
    return jnp.concatenate([ref[2 * t], ref[2 * t + 1]], axis=1)


def store_planes(upper_ref, lower_ref, start, codes, step, step256):
    count = codes.shape[0]
    rows = pl.ds(pl.multiple_of(start, count), count)
    upper = (codes + 128) >> 8
    upper_ref[rows, :] = (upper.astype(f32) * step256).astype(bf16)
    lower_ref[rows, :] = ((codes - (upper << 8)).astype(f32) * step).astype(bf16)


def iterate(ones_ref, upper_ref, lower_ref, residual, start):
    chunks = upper_ref.shape[0] // (2 * BL)
    rows, rank = residual.shape

    def operator(direction):
        planes = two_planes(direction)

        def chunk(t, total):
            span = pl.ds(pl.multiple_of(t * 2 * BL, 2 * BL), 2 * BL)
            upper, lower = upper_ref[span, :], lower_ref[span, :]
            weighted = pair_of(ones_ref, t) * scores(planes, upper, lower)
            return total + combine(weighted, upper, lower)

        total = lax.fori_loop(0, chunks, chunk, jnp.zeros((2 * rows, rank), f32), unroll=4)
        return fold(total) + LAM * direction

    solution = start
    direction = residual
    norm_now = jnp.sum(residual * residual, axis=-1, keepdims=True)
    for iteration in range(ITERS):
        image = operator(direction)
        alpha = norm_now / (jnp.sum(direction * image, axis=-1, keepdims=True) + EPS)
        solution = solution + alpha * direction
        if iteration + 1 < ITERS:
            residual = residual - alpha * image
            norm_next = jnp.sum(residual * residual, axis=-1, keepdims=True)
            direction = residual + norm_next / (norm_now + EPS) * direction
            norm_now = norm_next
    return solution


def item_kernel(start_ref, ones_ref, right_ref, words_ref, out_ref, upper_ref, lower_ref, total_ref):
    source = pl.program_id(0)
    half = words_ref.shape[1] - 8
    per = half // (2 * BL)
    exponent = words_ref[0, half : half + 1, :]
    step = power_of_two(exponent)
    step256 = step * 256.0
    base = source * 2 * half
    planes = two_planes(start_ref[...])

    @pl.when(source == 0)
    def _():
        total_ref[...] = jnp.zeros_like(total_ref)

    for c in range(per):
        words = words_ref[0, c * 2 * BL : (c + 1) * 2 * BL, :]
        store_planes(upper_ref, lower_ref, base + c * 2 * BL, words >> 16, step, step256)
        store_planes(upper_ref, lower_ref, base + half + c * 2 * BL, (words << 16) >> 16, step, step256)
    for c in range(2 * per):
        t = source * 2 * per + c
        span = pl.ds(pl.multiple_of(base + c * 2 * BL, 2 * BL), 2 * BL)
        upper, lower = upper_ref[span, :], lower_ref[span, :]
        weighted = pair_of(right_ref, t) - pair_of(ones_ref, t) * scores(planes, upper, lower)
        total_ref[...] += combine(weighted, upper, lower)

    @pl.when(source == pl.num_programs(0) - 1)
    def _():
        start = start_ref[...]
        residual = fold(total_ref[...]) - LAM * start
        out_ref[...] = iterate(ones_ref, upper_ref, lower_ref, residual, start)


def solve_items(start, ones, right, words):
    sources, depth, rank = words.shape
    rows = start.shape[0]
    whole = 2 * (depth - 8) * sources
    ones = ones.reshape(-1, rows, BL)
    right = right.reshape(-1, rows, BL)
    fixed3 = pl.BlockSpec(ones.shape, lambda s: (0, 0, 0), pipeline_mode=pl.Buffered(1))
    return pl.pallas_call(
        item_kernel,
        grid=(sources,),
        out_shape=jax.ShapeDtypeStruct((rows, rank), f32),
        in_specs=[
            pl.BlockSpec((rows, rank), lambda s: (0, 0)),
            fixed3,
            fixed3,
            pl.BlockSpec((1, depth, rank), lambda s: (s, 0, 0)),
        ],
        out_specs=pl.BlockSpec((rows, rank), lambda s: (0, 0)),
        scratch_shapes=[
            pltpu.VMEM((whole, rank), bf16),
            pltpu.VMEM((whole, rank), bf16),
            pltpu.VMEM((2 * rows, rank), f32),
        ],
        compiler_params=params(),
        name="solve_items",
    )(start, ones, right, words)


def held_kernel(
    core_ref, ones_ref, right_ref, own_ref, other_ref, out_ref, upper_ref, lower_ref, total_ref
):
    source = pl.program_id(0)
    half = own_ref.shape[1] - 16
    lanes = BL // 2
    blocks = half // lanes
    core = core_ref[0]

    @pl.when(source == 0)
    def _():
        total_ref[...] = jnp.zeros_like(total_ref)

    for ref, which in ((own_ref, core), (other_ref, 1 - core)):
        exponent = ref[0, half : half + 16, :].astype(i32)[:1]
        step = power_of_two(exponent)
        step256 = step * 256.0
        for b in range(blocks):
            codes = ref[0, b * lanes : (b + 1) * lanes, :].astype(i32)
            start = (source * blocks + b) * BL + which * lanes
            store_planes(upper_ref, lower_ref, start, codes, step, step256)
    for c in range(blocks // 2):
        t = source * (blocks // 2) + c
        span = pl.ds(pl.multiple_of(t * 2 * BL, 2 * BL), 2 * BL)
        total_ref[...] += combine(pair_of(right_ref, t), upper_ref[span, :], lower_ref[span, :])

    @pl.when(source == pl.num_programs(0) - 1)
    def _():
        residual = fold(total_ref[...])
        out_ref[...] = iterate(ones_ref, upper_ref, lower_ref, residual, jnp.zeros_like(residual))


def solve_held(core, ones, right, own, other, rows):
    sources, depth, rank = own.shape
    whole = 2 * (depth - 16) * sources
    ones = ones.reshape(-1, rows, BL)
    right = right.reshape(-1, rows, BL)
    fixed3 = pl.BlockSpec(ones.shape, lambda s: (0, 0, 0), pipeline_mode=pl.Buffered(1))
    codes = pl.BlockSpec((1, depth, rank), lambda s: (s, 0, 0))
    return pl.pallas_call(
        held_kernel,
        grid=(sources,),
        out_shape=jax.ShapeDtypeStruct((rows, rank), f32),
        in_specs=[pl.BlockSpec(memory_space=pltpu.SMEM), fixed3, fixed3, codes, codes],
        out_specs=pl.BlockSpec((rows, rank), lambda s: (0, 0)),
        scratch_shapes=[
            pltpu.VMEM((whole, rank), bf16),
            pltpu.VMEM((whole, rank), bf16),
            pltpu.VMEM((2 * rows, rank), f32),
        ],
        compiler_params=params(),
        name="solve_held",
    )(core, ones, right, own, other)


def with_codes(strips, codes):
    peers, _, lanes = strips.shape
    row = jnp.pad(codes.reshape(1, 1, -1), ((0, 0), (0, 15), (0, lanes - codes.size)))
    return jnp.concatenate([strips, jnp.broadcast_to(row.astype(bf16), (peers, 16, lanes))], axis=1)


def codes_of(received, slots):
    return received[:, -16, :slots].astype(i32).reshape(-1)


def shards(
    user_factors,
    item_factors,
    tile_user,
    tile_item,
    tile_count,
    tile_conf,
    held_user,
    held_item,
    held_count,
    held_conf,
):
    rank = user_factors.shape[1]
    peers = lax.axis_size("user")
    item_peers = lax.axis_size("item")
    chips = peers // 2
    me = lax.axis_index("user")
    core = me % 2
    chip = me // 2
    slots = tile_user.shape[-1]
    held_slots = held_user.shape[-1]
    user_blocks = user_factors.shape[0] // BL
    item_blocks = item_factors.shape[0] // BL
    held_blocks = 2

    words = lax.all_gather(pack_users(user_factors), "user", axis=0, tiled=False)

    live = jnp.arange(slots, dtype=i32)[None, :] < tile_count[0, 0][:, None]
    owner = jnp.arange(peers, dtype=i32)[:, None] * user_blocks
    code = jnp.where(live, (owner + tile_user[0, 0]) * item_blocks + tile_item[0, 0], peers * user_blocks * item_blocks)
    strips = tile_conf[0, 0].reshape(peers * slots, BL, 2, chips, SUB).transpose(3, 2, 0, 4, 1)
    strips = with_codes(strips.reshape(peers, peers * slots * SUB, BL), code)
    strips = lax.all_to_all(strips, "user", 0, 0, tiled=True)
    ones, right = dense(
        codes_of(strips, peers * slots), strips, peers * user_blocks * item_blocks, peers * slots, "dense_items"
    )

    held_live = jnp.arange(held_slots, dtype=i32)[None, :] < held_count[0, 0][:, None]
    held_owner = jnp.arange(item_peers, dtype=i32)[:, None] * item_blocks
    held_code = jnp.where(
        held_live, (held_owner + held_item[0, 0]) * held_blocks + held_user[0, 0], item_peers * item_blocks * held_blocks
    )
    held_strips = held_conf[0, 0].reshape(item_peers * held_slots, item_peers, SUB, BL).transpose(1, 0, 2, 3)
    held_strips = with_codes(held_strips.reshape(item_peers, item_peers * held_slots * SUB, BL), held_code)
    held_strips = lax.all_to_all(held_strips, "item", 0, 0, tiled=True)
    held_ones, held_right = dense(
        codes_of(held_strips, item_peers * held_slots),
        held_strips,
        item_peers * item_blocks * held_blocks,
        item_peers * held_slots,
        "dense_held",
    )

    start = lax.dynamic_slice_in_dim(
        item_factors.reshape(item_blocks, peers, SUB, rank), core * chips + chip, 1, axis=1
    ).reshape(item_blocks * SUB, rank)
    mine = solve_items(start, ones, right, words)

    same_core = [[c + 2 * z for z in range(chips)] for c in range(2)]
    siblings = [(d, d ^ 1) for d in range(peers)]
    half = lax.all_to_all(
        jnp.broadcast_to(mine[None], (chips,) + mine.shape), "user", 0, 0, tiled=True, axis_index_groups=same_core
    )
    own = lax.all_gather(pack_items(half), "item", axis=0, tiled=False)
    other = lax.ppermute(own, "user", siblings)
    folded = solve_held(core.reshape(1), held_ones, held_right, own, other, held_blocks * SUB)
    folded = lax.all_to_all(
        jnp.broadcast_to(folded[None], (item_peers,) + folded.shape), "item", 0, 0, tiled=True
    )
    folded = folded.reshape(item_peers, held_blocks, SUB, rank).transpose(1, 0, 2, 3).reshape(-1, rank)

    half = half.reshape(chips, item_blocks, SUB, rank).transpose(1, 0, 2, 3).reshape(item_blocks, 1, BL // 2, rank)
    sibling = lax.ppermute(half, "user", siblings)
    new_items = jnp.where(
        core == 0, jnp.concatenate([half, sibling], axis=1), jnp.concatenate([sibling, half], axis=1)
    ).reshape(-1, rank)
    return new_items, folded


def solution(mesh):
    in_specs = (
        P("user", None),
        P("item", None),
        P("item", "user", None, None),
        P("item", "user", None, None),
        P("item", "user", None),
        P("item", "user", None, None, None, None),
        P("user", "item", None, None),
        P("user", "item", None, None),
        P("user", "item", None),
        P("user", "item", None, None, None, None),
    )
    out_specs = (P("item", None), P("user", None))
    return jax.shard_map(shards, mesh=mesh, in_specs=in_specs, out_specs=out_specs, check_vma=False)
```

```python
import functools

import jax
import jax.numpy as jnp
from jax import lax
from jax.experimental import pallas as pl
from jax.experimental.pallas import tpu as pltpu
from jax.sharding import PartitionSpec as P

ITERS = 2
LAM = 1.0
EPS = 1e-6
BL = 128
SUB = 8
VMEM = 28 * 1024 * 1024

i32 = jnp.int32
f32 = jnp.float32
bf16 = jnp.bfloat16


def params():
    return pltpu.CompilerParams(vmem_limit_bytes=VMEM)


def vspec():
    return pl.BlockSpec(memory_space=pltpu.VMEM)


def power_of_two(exponent):
    bits = exponent + 126
    value = jnp.full(exponent.shape, 2.0**-126, f32)
    for k, power in enumerate((1, 2, 4, 8, 16, 32, 64)):
        value = value * jnp.where((bits >> k) & 1 == 1, f32(2.0**power), f32(1.0))
    high = jnp.where(bits >= 128, f32(2.0**64), f32(1.0))
    return value * high * high


def column_exponents(peak):
    rest = jnp.clip(peak, 2.0**-45, 2.0**60) * f32(2.0**60)
    found = jnp.zeros(peak.shape, i32)
    for k in (64, 32, 16, 8, 4, 2, 1):
        big = rest >= f32(2.0**k)
        rest = jnp.where(big, rest * f32(2.0**-k), rest)
        found = found + jnp.where(big, k, 0)
    return found - 74


def fixed_point(rows, inverse_step):
    return jnp.clip(jnp.round(rows * inverse_step), -32767.0, 32767.0).astype(i32)


def pack_users_kernel(place_ref, rows_ref, out_ref, exponent_ref):
    exponent = column_exponents(jnp.max(jnp.abs(rows_ref[...]), axis=0, keepdims=True))
    peers, part, rank = out_ref.shape
    first = pl.multiple_of(place_ref[0] * part, part)
    codes = fixed_point(rows_ref[pl.ds(first, part), :], power_of_two(-exponent)).astype(jnp.int16)
    for z in range(peers):
        out_ref[z] = codes
    exponent_ref[...] = exponent.astype(f32)


def pack_users(rows, place, peers, part):
    rank = rows.shape[1]
    return pl.pallas_call(
        pack_users_kernel,
        out_shape=(jax.ShapeDtypeStruct((peers, part, rank), jnp.int16), jax.ShapeDtypeStruct((1, rank), f32)),
        in_specs=[pl.BlockSpec(memory_space=pltpu.SMEM), vspec()],
        out_specs=(vspec(), vspec()),
        name="pack_users",
    )(place.reshape(1), rows)


def strips_kernel(turn, order, owner_scale, slot_scale, dead, place_ref, outer_ref, inner_ref, count_ref, tiles_ref, extra_ref, out_ref):
    owners, slots = outer_ref.shape
    total = owners * slots
    for t in range(0, total, 2):
        pair = [tiles_ref[t + k].astype(f32) for k in range(2)]
        if turn:
            pair = [tile.T for tile in pair]
        for d in range(len(order)):
            q = order[d] * SUB
            both = jnp.concatenate([pair[0][q : q + SUB], pair[1][q : q + SUB]], axis=0)
            out_ref[d, t * SUB : (t + 2) * SUB, :] = both.astype(bf16)
    outer_scale, owner_scale = owner_scale
    per = BL // total
    row = lax.broadcasted_iota(i32, (16, BL), 0)
    lane = lax.broadcasted_iota(i32, (16, BL), 1)
    place = place_ref[0]
    mine = jnp.where(row == place // per, lane - lax.rem(place, per) * total, -1)
    codes = jnp.zeros((16, BL), f32)
    for o in range(owners):
        for c in range(slots):
            code = (outer_ref[o, c] * outer_scale + o * owner_scale) * slot_scale + inner_ref[o, c]
            code = jnp.where(c < count_ref[o], code, dead)
            codes = jnp.where(mine == o * slots + c, code.astype(f32), codes)
    below = owners * total // BL
    for k in range(extra_ref.shape[1] // BL):
        codes = jnp.where(row == below + k, extra_ref[:, k * BL : (k + 1) * BL], codes)
    codes = codes.astype(bf16)
    for d in range(len(order)):
        out_ref[d, total * SUB :, :] = codes


def cut_strips(place, outer, inner, count, tiles, extra, turn, order, owner_scale, slot_scale, dead, name):
    owners, slots = outer.shape
    smem = pl.BlockSpec(memory_space=pltpu.SMEM)
    return pl.pallas_call(
        functools.partial(strips_kernel, turn, order, owner_scale, slot_scale, dead),
        out_shape=jax.ShapeDtypeStruct((len(order), owners * slots * SUB + 16, BL), bf16),
        in_specs=[smem, smem, smem, smem, vspec(), vspec()],
        out_specs=vspec(),
        compiler_params=params(),
        cost_estimate=pl.CostEstimate(flops=10**6, bytes_accessed=2 * 10**6, transcendentals=0),
        name=name,
    )(place.reshape(1), outer, inner, count, tiles.reshape(-1, BL, BL), extra)


def pack_items_kernel(rows_ref, out_ref):
    peers, rows, rank = rows_ref.shape
    blocks = rows // SUB
    peak = jnp.max(jnp.max(jnp.abs(rows_ref[...]), axis=0), axis=0, keepdims=True)
    exponent = column_exponents(peak)
    inverse = power_of_two(-exponent)
    for b in range(blocks):
        for z in range(0, peers, 2):
            pair = jnp.concatenate(
                [rows_ref[z, b * SUB : (b + 1) * SUB, :], rows_ref[z + 1, b * SUB : (b + 1) * SUB, :]], axis=0
            )
            start = (b * peers + z) * SUB
            out_ref[start : start + 2 * SUB, :] = fixed_point(pair, inverse).astype(jnp.int16)
    out_ref[peers * rows :, :] = jnp.broadcast_to(exponent, (16, rank)).astype(jnp.int16)


def pack_items(rows):
    peers, count, rank = rows.shape
    return pl.pallas_call(
        pack_items_kernel,
        out_shape=jax.ShapeDtypeStruct((peers * count + 16, rank), jnp.int16),
        in_specs=[vspec()],
        out_specs=vspec(),
        name="pack_items",
    )(rows)


def dense_kernel(blocks, slots, strips_ref, ones_ref, right_ref, step_ref, wide_ref):
    sources, depth, _ = strips_ref.shape
    count = slots * SUB
    table = strips_ref[0, count:depth, :].astype(f32)
    for s in range(1, sources):
        table = table + strips_ref[s, count:depth, :].astype(f32)
    held = sources * slots // BL
    codes = jnp.concatenate([table[k : k + 1, :] for k in range(held)], axis=1).astype(i32)
    rows = [strips_ref[s, count:depth, :].astype(f32) for s in range(sources)]
    rows = [jnp.concatenate([row[held : held + 1], row[held + 1 : held + 2]], axis=1) for row in rows]
    step_ref[...] = power_of_two(jnp.concatenate(rows, axis=0).astype(i32))
    named = lax.broadcasted_iota(i32, (blocks, sources * slots), 0) == codes
    named = jnp.where(named, f32(1.0), f32(0.0))
    live = jnp.sum(named, axis=1, keepdims=True)
    named = named.astype(bf16)
    for s in range(sources):
        wide_ref[s * count : (s + 1) * count, :] = strips_ref[s, :count, :].astype(f32)
    for r in range(SUB):
        rows = wide_ref[pl.ds(r, sources * slots, stride=SUB), :].astype(bf16)
        total = jnp.dot(named, rows, preferred_element_type=f32)
        ones_ref[pl.ds(r, blocks, stride=SUB), :] = total + 1.0
        right_ref[pl.ds(r, blocks, stride=SUB), :] = total + live


def dense(strips, blocks, slots, name):
    shape = jax.ShapeDtypeStruct((blocks * SUB, BL), f32)
    return pl.pallas_call(
        functools.partial(dense_kernel, blocks, slots),
        out_shape=(shape, shape, jax.ShapeDtypeStruct((strips.shape[0], 2 * BL), f32)),
        in_specs=[vspec()],
        out_specs=(vspec(), vspec(), vspec()),
        scratch_shapes=[pltpu.VMEM((strips.shape[0] * slots * SUB, BL), f32)],
        compiler_params=params(),
        cost_estimate=pl.CostEstimate(flops=4 * 10**8, bytes_accessed=3 * 10**6, transcendentals=0),
        name=name,
    )(strips)


NT = (((1,), (1,)), ((), ()))
NN = (((1,), (0,)), ((), ()))


def two_planes(value):
    upper = value.astype(bf16)
    return jnp.concatenate([upper, (value - upper.astype(f32)).astype(bf16)], axis=0)


def fold(both):
    rows = both.shape[0] // 2
    return both[:rows] + both[rows:]


def scores(direction, upper, lower):
    return fold(
        lax.dot_general(direction, upper, NT, preferred_element_type=f32)
        + lax.dot_general(direction, lower, NT, preferred_element_type=f32)
    )


def combine(weighted, upper, lower):
    planes = two_planes(weighted)
    return lax.dot_general(planes, upper, NN, preferred_element_type=f32) + lax.dot_general(
        planes, lower, NN, preferred_element_type=f32
    )


def columns(ref, first, count):
    return jnp.concatenate([ref[first + k] for k in range(count)], axis=1)


def high_part(codes):
    return (codes & -256).astype(f32)


def low_part(codes):
    return (codes & 255).astype(f32)


def iterate(ones_ref, upper_ref, lower_ref, residual, start):
    rows, rank = residual.shape
    group = 16 * BL
    steps = upper_ref.shape[0] // group

    def part(g, planes):
        span = pl.ds(pl.multiple_of(g * group, group), group)
        upper, lower = upper_ref[span, :], lower_ref[span, :]
        score = scores(planes, upper, lower)
        return score, columns(ones_ref, g * 16, 16) * score, upper, lower

    def operator(direction):
        planes = two_planes(direction)

        def step(g, total):
            _, weighted, upper, lower = part(g, planes)
            return total + combine(weighted, upper, lower)

        total = lax.fori_loop(0, steps, step, jnp.zeros((2 * rows, rank), f32))
        return fold(total) + LAM * direction

    def energy(direction):
        planes = two_planes(direction)

        def step(g, total):
            score, weighted, _, _ = part(g, planes)
            return total + jnp.sum(score * weighted, axis=-1, keepdims=True)

        total = lax.fori_loop(0, steps, step, jnp.zeros((rows, 1), f32))
        return total + LAM * jnp.sum(direction * direction, axis=-1, keepdims=True)

    solution = start
    direction = residual
    norm_now = jnp.sum(residual * residual, axis=-1, keepdims=True)
    for iteration in range(ITERS):
        if iteration + 1 == ITERS:
            return solution + norm_now / (energy(direction) + EPS) * direction
        image = operator(direction)
        alpha = norm_now / (jnp.sum(direction * image, axis=-1, keepdims=True) + EPS)
        solution = solution + alpha * direction
        residual = residual - alpha * image
        norm_next = jnp.sum(residual * residual, axis=-1, keepdims=True)
        direction = residual + norm_next / (norm_now + EPS) * direction
        norm_now = norm_next


def item_kernel(start_ref, ones_ref, right_ref, step_ref, core_ref, own_ref, other_ref, out_ref, upper_ref, lower_ref, total_ref):
    g = pl.program_id(0)
    parts, depth, _ = own_ref.shape
    part = BL // parts
    chips = depth // part
    group = chips * 2 * BL
    core = core_ref[0]
    planes = two_planes(start_ref[...])

    @pl.when(g == 0)
    def _():
        total_ref[...] = jnp.zeros_like(total_ref)

    for ref, which in ((own_ref, core), (other_ref, 1 - core)):
        for z in range(chips):
            step = step_ref[pl.ds(2 * z + which, 1), :]
            for k in range(parts):
                codes = ref[k, z * part : (z + 1) * part, :].astype(i32)
                rows = pl.ds(pl.multiple_of(g * group + (2 * z + which) * BL + k * part, part), part)
                upper_ref[rows, :] = (high_part(codes) * step).astype(bf16)
                lower_ref[rows, :] = (low_part(codes) * step).astype(bf16)
    span = pl.ds(pl.multiple_of(g * group, group), group)
    upper, lower = upper_ref[span, :], lower_ref[span, :]
    count = group // BL
    weighted = columns(right_ref, g * count, count) - columns(ones_ref, g * count, count) * scores(planes, upper, lower)
    total_ref[...] += combine(weighted, upper, lower)

    @pl.when(g == pl.num_programs(0) - 1)
    def _():
        start = start_ref[...]
        residual = fold(total_ref[...]) - LAM * start
        out_ref[...] = iterate(ones_ref, upper_ref, lower_ref, residual, start)


def solve_items(start, ones, right, step, core, own, other, user_blocks):
    sources, depth, rank = own.shape
    rows = start.shape[0]
    whole = 2 * depth * sources
    ones = ones.reshape(-1, rows, BL)
    right = right.reshape(-1, rows, BL)
    fixed3 = pl.BlockSpec(ones.shape, lambda s: (0, 0, 0), pipeline_mode=pl.Buffered(1))
    codes = pl.BlockSpec((sources // user_blocks, depth, rank), lambda s: (s, 0, 0))
    return pl.pallas_call(
        item_kernel,
        grid=(user_blocks,),
        out_shape=jax.ShapeDtypeStruct((rows, rank), f32),
        in_specs=[
            pl.BlockSpec((rows, rank), lambda s: (0, 0)),
            fixed3,
            fixed3,
            pl.BlockSpec(step.shape, lambda s: (0, 0)),
            pl.BlockSpec(memory_space=pltpu.SMEM),
            codes,
            codes,
        ],
        out_specs=pl.BlockSpec((rows, rank), lambda s: (0, 0)),
        scratch_shapes=[
            pltpu.VMEM((whole, rank), bf16),
            pltpu.VMEM((whole, rank), bf16),
            pltpu.VMEM((2 * rows, rank), f32),
        ],
        compiler_params=params(),
        cost_estimate=pl.CostEstimate(flops=12 * 10**9, bytes_accessed=10**7, transcendentals=0),
        name="solve_items",
    )(start, ones, right, step, core, own, other)


def held_kernel(
    core_ref, ones_ref, right_ref, own_ref, other_ref, out_ref, upper_ref, lower_ref, total_ref
):
    g = pl.program_id(0)
    sources, depth, _ = own_ref.shape
    half = depth - 16
    lanes = BL // 2
    blocks = half // lanes
    group = sources * 2 * half
    core = core_ref[0]

    @pl.when(g == 0)
    def _():
        total_ref[...] = jnp.zeros_like(total_ref)

    for s in range(sources):
        for ref, which in ((own_ref, core), (other_ref, 1 - core)):
            step = power_of_two(ref[s, half : half + 16, :].astype(i32)[:1])
            for b in range(blocks):
                codes = ref[s, b * lanes : (b + 1) * lanes, :].astype(i32)
                rows = pl.ds(pl.multiple_of(g * group + (s * blocks + b) * BL + which * lanes, lanes), lanes)
                upper_ref[rows, :] = (high_part(codes) * step).astype(bf16)
                lower_ref[rows, :] = (low_part(codes) * step).astype(bf16)
    span = pl.ds(pl.multiple_of(g * group, group), group)
    count = group // BL
    total_ref[...] += combine(columns(right_ref, g * count, count), upper_ref[span, :], lower_ref[span, :])

    @pl.when(g == pl.num_programs(0) - 1)
    def _():
        residual = fold(total_ref[...])
        out_ref[...] = iterate(ones_ref, upper_ref, lower_ref, residual, jnp.zeros_like(residual))


def solve_held(core, ones, right, own, other, rows):
    sources, depth, rank = own.shape
    whole = 2 * (depth - 16) * sources
    ones = ones.reshape(-1, rows, BL)
    right = right.reshape(-1, rows, BL)
    fixed3 = pl.BlockSpec(ones.shape, lambda s: (0, 0, 0), pipeline_mode=pl.Buffered(1))
    codes = pl.BlockSpec((4, depth, rank), lambda s: (s, 0, 0))
    return pl.pallas_call(
        held_kernel,
        grid=(sources // 4,),
        out_shape=jax.ShapeDtypeStruct((rows, rank), f32),
        in_specs=[pl.BlockSpec(memory_space=pltpu.SMEM), fixed3, fixed3, codes, codes],
        out_specs=pl.BlockSpec((rows, rank), lambda s: (0, 0)),
        scratch_shapes=[
            pltpu.VMEM((whole, rank), bf16),
            pltpu.VMEM((whole, rank), bf16),
            pltpu.VMEM((2 * rows, rank), f32),
        ],
        compiler_params=params(),
        name="solve_held",
    )(core, ones, right, own, other)


def shards(
    user_factors,
    item_factors,
    tile_user,
    tile_item,
    tile_count,
    tile_conf,
    held_user,
    held_item,
    held_count,
    held_conf,
):
    rank = user_factors.shape[1]
    peers = lax.axis_size("user")
    item_peers = lax.axis_size("item")
    chips = peers // 2
    me = lax.axis_index("user")
    core = me % 2
    chip = me // 2
    slots = tile_user.shape[-1]
    held_slots = held_user.shape[-1]
    user_blocks = user_factors.shape[0] // BL
    item_blocks = item_factors.shape[0] // BL
    held_blocks = 2

    same_core = [[c + 2 * z for z in range(chips)] for c in range(2)]
    siblings = [(d, d ^ 1) for d in range(peers)]

    part = user_factors.shape[0] // item_peers
    column = lax.axis_index("item")
    piece, exponent = pack_users(user_factors, column, chips, part)
    piece = lax.all_to_all(piece, "user", 0, 0, tiled=True, axis_index_groups=same_core).reshape(chips * part, rank)

    blocks = peers * user_blocks * item_blocks
    order = [c * chips + z for z in range(chips) for c in range(2)]
    strips = cut_strips(
        me, tile_user[0, 0], tile_item[0, 0], tile_count[0, 0], tile_conf, exponent,
        True, order, (peers, 1), item_blocks, blocks, "cut_items",
    )
    held_all = item_peers * item_blocks * held_blocks
    held_strips = cut_strips(
        column, held_item[0, 0], held_user[0, 0], held_count[0, 0], held_conf, jnp.zeros_like(exponent),
        False, list(range(item_peers)), (1, item_blocks), held_blocks, held_all, "cut_held",
    )
    strips, held_strips, piece = lax.optimization_barrier((strips, held_strips, piece))
    strips = lax.all_to_all(strips, "user", 0, 0, tiled=True)
    own_users = lax.all_gather(piece, "item", axis=0, tiled=False)
    strips, own_users, held_strips = lax.optimization_barrier((strips, own_users, held_strips))
    other_users = lax.ppermute(own_users, "user", siblings)
    held_strips = lax.all_to_all(held_strips, "item", 0, 0, tiled=True)
    ones, right, step = dense(strips, blocks, peers * slots, "dense_items")

    start = lax.dynamic_slice_in_dim(
        item_factors.reshape(item_blocks, peers, SUB, rank), core * chips + chip, 1, axis=1
    ).reshape(item_blocks * SUB, rank)
    mine = solve_items(start, ones, right, step, core.reshape(1), own_users, other_users, user_blocks)
    mine, held_strips = lax.optimization_barrier((mine, held_strips))
    held_ones, held_right, _ = dense(held_strips, held_all, item_peers * held_slots, "dense_held")

    half = lax.all_to_all(
        jnp.broadcast_to(mine[None], (chips,) + mine.shape), "user", 0, 0, tiled=True, axis_index_groups=same_core
    )
    own = lax.all_gather(pack_items(half), "item", axis=0, tiled=False)
    other = lax.ppermute(own, "user", siblings)
    folded = solve_held(core.reshape(1), held_ones, held_right, own, other, held_blocks * SUB)
    folded = lax.all_to_all(
        jnp.broadcast_to(folded[None], (item_peers,) + folded.shape), "item", 0, 0, tiled=True
    )
    folded = folded.reshape(item_peers, held_blocks, SUB, rank).transpose(1, 0, 2, 3).reshape(-1, rank)

    half = half.reshape(chips, item_blocks, SUB, rank).transpose(1, 0, 2, 3).reshape(item_blocks, 1, BL // 2, rank)
    sibling = lax.ppermute(half, "user", siblings)
    new_items = jnp.where(
        core == 0, jnp.concatenate([half, sibling], axis=1), jnp.concatenate([sibling, half], axis=1)
    ).reshape(-1, rank)
    return new_items, folded


def solution(mesh):
    in_specs = (
        P("user", None),
        P("item", None),
        P("item", "user", None, None),
        P("item", "user", None, None),
        P("item", "user", None),
        P("item", "user", None, None, None, None),
        P("user", "item", None, None),
        P("user", "item", None, None),
        P("user", "item", None),
        P("user", "item", None, None, None, None),
    )
    out_specs = (P("item", None), P("user", None))
    return jax.shard_map(shards, mesh=mesh, in_specs=in_specs, out_specs=out_specs, check_vma=False)
```

```python
import functools

import jax
import jax.numpy as jnp
from jax import lax
from jax.experimental import pallas as pl
from jax.experimental.pallas import tpu as pltpu
from jax.sharding import PartitionSpec as P

ITERS = 2
LAM = 1.0
EPS = 1e-6
BL = 128
SUB = 8
GROUP = 32
VMEM = 28 * 1024 * 1024

i32 = jnp.int32
f32 = jnp.float32
bf16 = jnp.bfloat16


def params():
    return pltpu.CompilerParams(vmem_limit_bytes=VMEM)


def vspec():
    return pl.BlockSpec(memory_space=pltpu.VMEM)


def power_of_two(exponent):
    bits = exponent + 126
    value = jnp.full(exponent.shape, 2.0**-126, f32)
    for k, power in enumerate((1, 2, 4, 8, 16, 32, 64)):
        value = value * jnp.where((bits >> k) & 1 == 1, f32(2.0**power), f32(1.0))
    high = jnp.where(bits >= 128, f32(2.0**64), f32(1.0))
    return value * high * high


def column_exponents(peak):
    rest = jnp.clip(peak, 2.0**-45, 2.0**60) * f32(2.0**60)
    found = jnp.zeros(peak.shape, i32)
    for k in (64, 32, 16, 8, 4, 2, 1):
        big = rest >= f32(2.0**k)
        rest = jnp.where(big, rest * f32(2.0**-k), rest)
        found = found + jnp.where(big, k, 0)
    return found - 74


def fixed_point(rows, inverse_step):
    return jnp.clip(jnp.round(rows * inverse_step), -32767.0, 32767.0).astype(i32)


def pack_users_kernel(place_ref, rows_ref, out_ref, exponent_ref):
    exponent = column_exponents(jnp.max(jnp.abs(rows_ref[...]), axis=0, keepdims=True))
    peers, part, rank = out_ref.shape
    first = pl.multiple_of(place_ref[0] * part, part)
    codes = fixed_point(rows_ref[pl.ds(first, part), :], power_of_two(-exponent)).astype(jnp.int16)
    for z in range(peers):
        out_ref[z] = codes
    exponent_ref[...] = exponent.astype(f32)


def pack_users(rows, place, peers, part):
    rank = rows.shape[1]
    return pl.pallas_call(
        pack_users_kernel,
        out_shape=(jax.ShapeDtypeStruct((peers, part, rank), jnp.int16), jax.ShapeDtypeStruct((1, rank), f32)),
        in_specs=[pl.BlockSpec(memory_space=pltpu.SMEM), vspec()],
        out_specs=(vspec(), vspec()),
        name="pack_users",
    )(place.reshape(1), rows)


def strips_kernel(turn, order, owner_scale, slot_scale, dead, place_ref, outer_ref, inner_ref, count_ref, tiles_ref, extra_ref, out_ref):
    slots, owners = outer_ref.shape
    total = owners * slots
    for t in range(0, total, 2):
        pair = [tiles_ref[t + k].astype(f32) for k in range(2)]
        if turn:
            pair = [tile.T for tile in pair]
        for d in range(len(order)):
            q = order[d] * SUB
            both = jnp.concatenate([pair[0][q : q + SUB], pair[1][q : q + SUB]], axis=0)
            out_ref[d, t * SUB : (t + 2) * SUB, :] = both.astype(bf16)
    outer_scale, owner_scale = owner_scale
    per = BL // total
    row = lax.broadcasted_iota(i32, (16, BL), 0)
    lane = lax.broadcasted_iota(i32, (16, BL), 1)
    place = place_ref[0]
    mine = jnp.where(row == place // per, lane - lax.rem(place, per) * total, -1)
    codes = jnp.zeros((16, BL), f32)
    for o in range(owners):
        for c in range(slots):
            code = (outer_ref[c, o] * outer_scale + o * owner_scale) * slot_scale + inner_ref[c, o]
            code = jnp.where(c < count_ref[o], code, dead)
            codes = jnp.where(mine == o * slots + c, code.astype(f32), codes)
    below = owners * total // BL
    for k in range(extra_ref.shape[1] // BL):
        codes = jnp.where(row == below + k, extra_ref[:, k * BL : (k + 1) * BL], codes)
    codes = codes.astype(bf16)
    for d in range(len(order)):
        out_ref[d, total * SUB :, :] = codes


def cut_strips(place, outer, inner, count, tiles, extra, turn, order, owner_scale, slot_scale, dead, name):
    slots, owners = outer.shape
    smem = pl.BlockSpec(memory_space=pltpu.SMEM)
    return pl.pallas_call(
        functools.partial(strips_kernel, turn, order, owner_scale, slot_scale, dead),
        out_shape=jax.ShapeDtypeStruct((len(order), owners * slots * SUB + 16, BL), bf16),
        in_specs=[smem, smem, smem, smem, vspec(), vspec()],
        out_specs=vspec(),
        compiler_params=params(),
        cost_estimate=pl.CostEstimate(flops=10**6, bytes_accessed=2 * 10**6, transcendentals=0),
        name=name,
    )(place.reshape(1), outer, inner, count, tiles.reshape(-1, BL, BL), extra)


def pack_items_kernel(rows_ref, out_ref):
    peers, rows, rank = rows_ref.shape
    blocks = rows // SUB
    peak = jnp.max(jnp.max(jnp.abs(rows_ref[...]), axis=0), axis=0, keepdims=True)
    exponent = column_exponents(peak)
    inverse = power_of_two(-exponent)
    for b in range(blocks):
        for z in range(0, peers, 2):
            pair = jnp.concatenate(
                [rows_ref[z, b * SUB : (b + 1) * SUB, :], rows_ref[z + 1, b * SUB : (b + 1) * SUB, :]], axis=0
            )
            start = (b * peers + z) * SUB
            out_ref[start : start + 2 * SUB, :] = fixed_point(pair, inverse).astype(jnp.int16)
    out_ref[peers * rows :, :] = jnp.broadcast_to(exponent, (16, rank)).astype(jnp.int16)


def pack_items(rows):
    peers, count, rank = rows.shape
    return pl.pallas_call(
        pack_items_kernel,
        out_shape=jax.ShapeDtypeStruct((peers * count + 16, rank), jnp.int16),
        in_specs=[vspec()],
        out_specs=vspec(),
        name="pack_items",
    )(rows)


def dense_kernel(blocks, slots, strips_ref, ones_ref, right_ref, step_ref, wide_ref):
    sources, depth, _ = strips_ref.shape
    count = slots * SUB
    table = strips_ref[0, count:depth, :].astype(f32)
    for s in range(1, sources):
        table = table + strips_ref[s, count:depth, :].astype(f32)
    held = sources * slots // BL
    codes = jnp.concatenate([table[k : k + 1, :] for k in range(held)], axis=1).astype(i32)
    rows = [strips_ref[s, count:depth, :].astype(f32) for s in range(sources)]
    rows = [jnp.concatenate([row[held : held + 1], row[held + 1 : held + 2]], axis=1) for row in rows]
    step_ref[...] = power_of_two(jnp.concatenate(rows, axis=0).astype(i32))
    named = lax.broadcasted_iota(i32, (blocks, sources * slots), 0) == codes
    named = jnp.where(named, f32(1.0), f32(0.0))
    live = jnp.sum(named, axis=1, keepdims=True)
    named = named.astype(bf16)
    for s in range(sources):
        wide_ref[s * count : (s + 1) * count, :] = strips_ref[s, :count, :].astype(f32)
    for r in range(SUB):
        rows = wide_ref[pl.ds(r, sources * slots, stride=SUB), :].astype(bf16)
        total = jnp.dot(named, rows, preferred_element_type=f32)
        ones_ref[pl.ds(r, blocks, stride=SUB), :] = total + 1.0
        right_ref[pl.ds(r, blocks, stride=SUB), :] = total + live


def dense(strips, blocks, slots, name):
    shape = jax.ShapeDtypeStruct((blocks * SUB, BL), f32)
    return pl.pallas_call(
        functools.partial(dense_kernel, blocks, slots),
        out_shape=(shape, shape, jax.ShapeDtypeStruct((strips.shape[0], 2 * BL), f32)),
        in_specs=[vspec()],
        out_specs=(vspec(), vspec(), vspec()),
        scratch_shapes=[pltpu.VMEM((strips.shape[0] * slots * SUB, BL), f32)],
        compiler_params=params(),
        cost_estimate=pl.CostEstimate(flops=4 * 10**8, bytes_accessed=3 * 10**6, transcendentals=0),
        name=name,
    )(strips)


NT = (((1,), (1,)), ((), ()))
NN = (((1,), (0,)), ((), ()))


def two_planes(value):
    upper = value.astype(bf16)
    return jnp.concatenate([upper, (value - upper.astype(f32)).astype(bf16)], axis=0)


def fold(both):
    rows = both.shape[0] // 2
    return both[:rows] + both[rows:]


def twice(planes):
    return jnp.concatenate([planes, planes], axis=1)


def scores(planes, factors):
    return fold(lax.dot_general(planes, factors, NT, preferred_element_type=f32))


def combine(weighted, factors):
    return jnp.dot(two_planes(weighted), factors, preferred_element_type=f32)


def join(both):
    rank = both.shape[1] // 2
    return fold(both[:, :rank] + both[:, rank:])


def columns(ref, first, count):
    return jnp.concatenate([ref[first + k] for k in range(count)], axis=1)


def high_part(codes):
    return (codes & -256).astype(f32)


def low_part(codes):
    return (codes & 255).astype(f32)


def iterate(ones_ref, factors_ref, residual, start):
    rows, rank = residual.shape
    group = GROUP * BL
    steps = factors_ref.shape[0] // group

    def part(g, planes):
        factors = factors_ref[pl.ds(pl.multiple_of(g * group, group), group), :]
        score = scores(planes, factors)
        return score, columns(ones_ref, g * GROUP, GROUP) * score, factors

    def operator(direction):
        planes = twice(two_planes(direction))

        def step(g, total):
            _, weighted, factors = part(g, planes)
            return total + combine(weighted, factors)

        total = lax.fori_loop(0, steps, step, jnp.zeros((2 * rows, 2 * rank), f32))
        return join(total) + LAM * direction

    def energy(direction):
        planes = twice(two_planes(direction))

        def step(g, total):
            score, weighted, _ = part(g, planes)
            return total + jnp.sum(score * weighted, axis=-1, keepdims=True)

        total = lax.fori_loop(0, steps, step, jnp.zeros((rows, 1), f32))
        return total + LAM * jnp.sum(direction * direction, axis=-1, keepdims=True)

    solution = start
    direction = residual
    norm_now = jnp.sum(residual * residual, axis=-1, keepdims=True)
    for iteration in range(ITERS):
        if iteration + 1 == ITERS:
            return solution + norm_now / (energy(direction) + EPS) * direction
        image = operator(direction)
        alpha = norm_now / (jnp.sum(direction * image, axis=-1, keepdims=True) + EPS)
        solution = solution + alpha * direction
        residual = residual - alpha * image
        norm_next = jnp.sum(residual * residual, axis=-1, keepdims=True)
        direction = residual + norm_next / (norm_now + EPS) * direction
        norm_now = norm_next


def item_kernel(chips, start_ref, ones_ref, right_ref, step_ref, core_ref, own_ref, other_ref, out_ref, factors_ref, total_ref):
    g = pl.program_id(0)
    sources, depth, rank = own_ref.shape
    part = depth // chips
    per = BL // part
    group = sources * 2 * depth
    core = core_ref[0]

    @pl.when(g == 0)
    def _():
        total_ref[...] = jnp.zeros_like(total_ref)

    for ref, which in ((own_ref, core), (other_ref, 1 - core)):
        for z in range(chips):
            step = step_ref[pl.ds(2 * z + which, 1), :]
            for k in range(sources):
                codes = ref[k, z * part : (z + 1) * part, :].astype(i32)
                start = g * group + (k // per * 2 * chips + 2 * z + which) * BL + k % per * part
                rows = pl.ds(pl.multiple_of(start, part), part)
                factors_ref[rows, :rank] = (high_part(codes) * step).astype(bf16)
                factors_ref[rows, rank:] = (low_part(codes) * step).astype(bf16)
    factors = factors_ref[pl.ds(pl.multiple_of(g * group, group), group), :]
    count = group // BL
    score = scores(twice(two_planes(start_ref[...])), factors)
    weighted = columns(right_ref, g * count, count) - columns(ones_ref, g * count, count) * score
    total_ref[...] += combine(weighted, factors)

    @pl.when(g == pl.num_programs(0) - 1)
    def _():
        start = start_ref[...]
        found = iterate(ones_ref, factors_ref, join(total_ref[...]) - LAM * start, start)
        for d in range(out_ref.shape[0]):
            out_ref[d] = found


def solve_items(start, ones, right, step, core, own, other, copies):
    sources, depth, rank = own.shape
    rows = start.shape[0]
    whole = 2 * depth * sources
    grid = whole // (GROUP * BL)
    ones = ones.reshape(-1, rows, BL)
    right = right.reshape(-1, rows, BL)
    fixed3 = pl.BlockSpec(ones.shape, lambda s: (0, 0, 0), pipeline_mode=pl.Buffered(1))
    codes = pl.BlockSpec((sources // grid, depth, rank), lambda s: (s, 0, 0))
    return pl.pallas_call(
        functools.partial(item_kernel, copies),
        grid=(grid,),
        out_shape=jax.ShapeDtypeStruct((copies, rows, rank), f32),
        in_specs=[
            pl.BlockSpec((rows, rank), lambda s: (0, 0)),
            fixed3,
            fixed3,
            pl.BlockSpec(step.shape, lambda s: (0, 0)),
            pl.BlockSpec(memory_space=pltpu.SMEM),
            codes,
            codes,
        ],
        out_specs=pl.BlockSpec((copies, rows, rank), lambda s: (0, 0, 0)),
        scratch_shapes=[pltpu.VMEM((whole, 2 * rank), bf16), pltpu.VMEM((2 * rows, 2 * rank), f32)],
        compiler_params=params(),
        cost_estimate=pl.CostEstimate(flops=12 * 10**9, bytes_accessed=10**7, transcendentals=0),
        name="solve_items",
    )(start, ones, right, step, core, own, other)


def held_kernel(core_ref, ones_ref, right_ref, own_ref, other_ref, out_ref, factors_ref, total_ref):
    g = pl.program_id(0)
    sources, depth, rank = own_ref.shape
    half = depth - 16
    lanes = BL // 2
    blocks = half // lanes
    group = sources * 2 * half
    core = core_ref[0]

    @pl.when(g == 0)
    def _():
        total_ref[...] = jnp.zeros_like(total_ref)

    for s in range(sources):
        for ref, which in ((own_ref, core), (other_ref, 1 - core)):
            step = power_of_two(ref[s, half : half + 16, :].astype(i32)[:1])
            for b in range(blocks):
                codes = ref[s, b * lanes : (b + 1) * lanes, :].astype(i32)
                start = g * group + (s * blocks + b) * BL + which * lanes
                rows = pl.ds(pl.multiple_of(start, lanes), lanes)
                factors_ref[rows, :rank] = (high_part(codes) * step).astype(bf16)
                factors_ref[rows, rank:] = (low_part(codes) * step).astype(bf16)
    factors = factors_ref[pl.ds(pl.multiple_of(g * group, group), group), :]
    count = group // BL
    total_ref[...] += combine(columns(right_ref, g * count, count), factors)

    @pl.when(g == pl.num_programs(0) - 1)
    def _():
        residual = join(total_ref[...])
        found = iterate(ones_ref, factors_ref, residual, jnp.zeros_like(residual))
        for d in range(out_ref.shape[0]):
            out_ref[d] = found


def solve_held(core, ones, right, own, other, rows, copies):
    sources, depth, rank = own.shape
    whole = 2 * (depth - 16) * sources
    grid = whole // (GROUP * BL)
    ones = ones.reshape(-1, rows, BL)
    right = right.reshape(-1, rows, BL)
    fixed3 = pl.BlockSpec(ones.shape, lambda s: (0, 0, 0), pipeline_mode=pl.Buffered(1))
    codes = pl.BlockSpec((sources // grid, depth, rank), lambda s: (s, 0, 0))
    return pl.pallas_call(
        held_kernel,
        grid=(grid,),
        out_shape=jax.ShapeDtypeStruct((copies, rows, rank), f32),
        in_specs=[pl.BlockSpec(memory_space=pltpu.SMEM), fixed3, fixed3, codes, codes],
        out_specs=pl.BlockSpec((copies, rows, rank), lambda s: (0, 0, 0)),
        scratch_shapes=[pltpu.VMEM((whole, 2 * rank), bf16), pltpu.VMEM((2 * rows, 2 * rank), f32)],
        compiler_params=params(),
        name="solve_held",
    )(core, ones, right, own, other)


def shards(
    user_factors,
    item_factors,
    tile_user,
    tile_item,
    tile_count,
    tile_conf,
    held_user,
    held_item,
    held_count,
    held_conf,
):
    rank = user_factors.shape[1]
    peers = lax.axis_size("user")
    item_peers = lax.axis_size("item")
    chips = peers // 2
    me = lax.axis_index("user")
    core = me % 2
    chip = me // 2
    slots = tile_user.shape[-1]
    held_slots = held_user.shape[-1]
    user_blocks = user_factors.shape[0] // BL
    item_blocks = item_factors.shape[0] // BL
    held_blocks = 2

    same_core = [[c + 2 * z for z in range(chips)] for c in range(2)]
    siblings = [(d, d ^ 1) for d in range(peers)]

    part = user_factors.shape[0] // item_peers
    column = lax.axis_index("item")
    piece, exponent = pack_users(user_factors, column, chips, part)
    piece = lax.all_to_all(piece, "user", 0, 0, tiled=True, axis_index_groups=same_core).reshape(chips * part, rank)

    blocks = peers * user_blocks * item_blocks
    order = [c * chips + z for z in range(chips) for c in range(2)]
    strips = cut_strips(
        me, tile_user[0, 0].T, tile_item[0, 0].T, tile_count[0, 0], tile_conf, exponent,
        True, order, (peers, 1), item_blocks, blocks, "cut_items",
    )
    held_all = item_peers * item_blocks * held_blocks
    held_strips = cut_strips(
        column, held_item[0, 0].T, held_user[0, 0].T, held_count[0, 0], held_conf, jnp.zeros_like(exponent),
        False, list(range(item_peers)), (1, item_blocks), held_blocks, held_all, "cut_held",
    )
    strips, held_strips, piece = lax.optimization_barrier((strips, held_strips, piece))
    strips = lax.all_to_all(strips, "user", 0, 0, tiled=True)
    own_users = lax.all_gather(piece, "item", axis=0, tiled=False)
    strips, own_users, held_strips = lax.optimization_barrier((strips, own_users, held_strips))
    other_users = lax.ppermute(own_users, "user", siblings)
    held_strips = lax.all_to_all(held_strips, "item", 0, 0, tiled=True)
    ones, right, step = dense(strips, blocks, peers * slots, "dense_items")

    start = lax.dynamic_slice_in_dim(
        item_factors.reshape(item_blocks, peers, SUB, rank), core * chips + chip, 1, axis=1
    ).reshape(item_blocks * SUB, rank)
    mine = solve_items(start, ones, right, step, core.reshape(1), own_users, other_users, chips)
    mine, held_strips = lax.optimization_barrier((mine, held_strips))
    held_ones, held_right, _ = dense(held_strips, held_all, item_peers * held_slots, "dense_held")

    half = lax.all_to_all(mine, "user", 0, 0, tiled=True, axis_index_groups=same_core)
    own = lax.all_gather(pack_items(half), "item", axis=0, tiled=False)
    other = lax.ppermute(own, "user", siblings)
    folded = solve_held(core.reshape(1), held_ones, held_right, own, other, held_blocks * SUB, item_peers)
    folded = lax.all_to_all(folded, "item", 0, 0, tiled=True)
    folded = folded.reshape(item_peers, held_blocks, SUB, rank).transpose(1, 0, 2, 3).reshape(-1, rank)

    half = half.reshape(chips, item_blocks, SUB, rank).transpose(1, 0, 2, 3).reshape(item_blocks, 1, BL // 2, rank)
    sibling = lax.ppermute(half, "user", siblings)
    new_items = jnp.where(
        core == 0, jnp.concatenate([half, sibling], axis=1), jnp.concatenate([sibling, half], axis=1)
    ).reshape(-1, rank)
    return new_items, folded


def solution(mesh):
    in_specs = (
        P("user", None),
        P("item", None),
        P("item", "user", None, None),
        P("item", "user", None, None),
        P("item", "user", None),
        P("item", "user", None, None, None, None),
        P("user", "item", None, None),
        P("user", "item", None, None),
        P("user", "item", None),
        P("user", "item", None, None, None, None),
    )
    out_specs = (P("item", None), P("user", None))
    return jax.shard_map(shards, mesh=mesh, in_specs=in_specs, out_specs=out_specs, check_vma=False)
```

```python
import functools

import jax
import jax.numpy as jnp
from jax import lax
from jax.experimental import pallas as pl
from jax.experimental.pallas import tpu as pltpu
from jax.sharding import PartitionSpec as P

ITERS = 2
LAM = 1.0
EPS = 1e-6
BL = 128
SUB = 8
GROUP = 32
USER = ("z", "c")
ITEM = ("y", "x")
VMEM = 28 * 1024 * 1024

i32 = jnp.int32
f32 = jnp.float32
bf16 = jnp.bfloat16


def params():
    return pltpu.CompilerParams(vmem_limit_bytes=VMEM)


def vspec():
    return pl.BlockSpec(memory_space=pltpu.VMEM)


def power_of_two(exponent):
    bits = exponent + 126
    value = jnp.full(exponent.shape, 2.0**-126, f32)
    for k, power in enumerate((1, 2, 4, 8, 16, 32, 64)):
        value = value * jnp.where((bits >> k) & 1 == 1, f32(2.0**power), f32(1.0))
    high = jnp.where(bits >= 128, f32(2.0**64), f32(1.0))
    return value * high * high


def column_exponents(peak):
    rest = jnp.clip(peak, 2.0**-45, 2.0**60) * f32(2.0**60)
    found = jnp.zeros(peak.shape, i32)
    for k in (64, 32, 16, 8, 4, 2, 1):
        big = rest >= f32(2.0**k)
        rest = jnp.where(big, rest * f32(2.0**-k), rest)
        found = found + jnp.where(big, k, 0)
    return found - 74


def fixed_point(rows, inverse_step):
    return jnp.clip(jnp.round(rows * inverse_step), -32767.0, 32767.0).astype(i32)


def pack_users_kernel(place_ref, rows_ref, out_ref, exponent_ref):
    exponent = column_exponents(jnp.max(jnp.abs(rows_ref[...]), axis=0, keepdims=True))
    peers, part, rank = out_ref.shape
    first = pl.multiple_of(place_ref[0] * part, part)
    codes = fixed_point(rows_ref[pl.ds(first, part), :], power_of_two(-exponent)).astype(jnp.int16)
    for z in range(peers):
        out_ref[z] = codes
    exponent_ref[...] = exponent.astype(f32)


def pack_users(rows, place, peers, part):
    rank = rows.shape[1]
    return pl.pallas_call(
        pack_users_kernel,
        out_shape=(jax.ShapeDtypeStruct((peers, part, rank), jnp.int16), jax.ShapeDtypeStruct((1, rank), f32)),
        in_specs=[pl.BlockSpec(memory_space=pltpu.SMEM), vspec()],
        out_specs=(vspec(), vspec()),
        name="pack_users",
    )(place.reshape(1), rows)


def strips_kernel(turn, order, owner_scale, slot_scale, dead, place_ref, outer_ref, inner_ref, count_ref, tiles_ref, extra_ref, out_ref):
    slots, owners = outer_ref.shape
    total = owners * slots
    for t in range(0, total, 2):
        pair = [tiles_ref[t + k].astype(f32) for k in range(2)]
        if turn:
            pair = [tile.T for tile in pair]
        for d in range(len(order)):
            q = order[d] * SUB
            both = jnp.concatenate([pair[0][q : q + SUB], pair[1][q : q + SUB]], axis=0)
            out_ref[d, t * SUB : (t + 2) * SUB, :] = both.astype(bf16)
    outer_scale, owner_scale = owner_scale
    per = BL // total
    row = lax.broadcasted_iota(i32, (16, BL), 0)
    lane = lax.broadcasted_iota(i32, (16, BL), 1)
    place = place_ref[0]
    mine = jnp.where(row == place // per, lane - lax.rem(place, per) * total, -1)
    codes = jnp.zeros((16, BL), f32)
    for o in range(owners):
        for c in range(slots):
            code = (outer_ref[c, o] * outer_scale + o * owner_scale) * slot_scale + inner_ref[c, o]
            code = jnp.where(c < count_ref[o], code, dead)
            codes = jnp.where(mine == o * slots + c, code.astype(f32), codes)
    below = owners * total // BL
    for k in range(extra_ref.shape[1] // BL):
        codes = jnp.where(row == below + k, extra_ref[:, k * BL : (k + 1) * BL], codes)
    codes = codes.astype(bf16)
    for d in range(len(order)):
        out_ref[d, total * SUB :, :] = codes


def cut_strips(place, outer, inner, count, tiles, extra, turn, order, owner_scale, slot_scale, dead, name):
    slots, owners = outer.shape
    smem = pl.BlockSpec(memory_space=pltpu.SMEM)
    return pl.pallas_call(
        functools.partial(strips_kernel, turn, order, owner_scale, slot_scale, dead),
        out_shape=jax.ShapeDtypeStruct((len(order), owners * slots * SUB + 16, BL), bf16),
        in_specs=[smem, smem, smem, smem, vspec(), vspec()],
        out_specs=vspec(),
        compiler_params=params(),
        cost_estimate=pl.CostEstimate(flops=10**6, bytes_accessed=2 * 10**6, transcendentals=0),
        name=name,
    )(place.reshape(1), outer, inner, count, tiles.reshape(-1, BL, BL), extra)


def dense_kernel(blocks, slots, strips_ref, ones_ref, right_ref, step_ref, wide_ref):
    sources, depth, _ = strips_ref.shape
    count = slots * SUB
    table = strips_ref[0, count:depth, :].astype(f32)
    for s in range(1, sources):
        table = table + strips_ref[s, count:depth, :].astype(f32)
    held = sources * slots // BL
    codes = jnp.concatenate([table[k : k + 1, :] for k in range(held)], axis=1).astype(i32)
    rows = [strips_ref[s, count:depth, :].astype(f32) for s in range(sources)]
    rows = [jnp.concatenate([row[held : held + 1], row[held + 1 : held + 2]], axis=1) for row in rows]
    step_ref[...] = power_of_two(jnp.concatenate(rows, axis=0).astype(i32))
    named = lax.broadcasted_iota(i32, (blocks, sources * slots), 0) == codes
    named = jnp.where(named, f32(1.0), f32(0.0))
    live = jnp.sum(named, axis=1, keepdims=True)
    named = named.astype(bf16)
    for s in range(sources):
        wide_ref[s * count : (s + 1) * count, :] = strips_ref[s, :count, :].astype(f32)
    for r in range(SUB):
        rows = wide_ref[pl.ds(r, sources * slots, stride=SUB), :].astype(bf16)
        total = jnp.dot(named, rows, preferred_element_type=f32)
        ones_ref[pl.ds(r, blocks, stride=SUB), :] = total + 1.0
        right_ref[pl.ds(r, blocks, stride=SUB), :] = total + live


def dense(strips, blocks, slots, name):
    shape = jax.ShapeDtypeStruct((blocks * SUB, BL), f32)
    return pl.pallas_call(
        functools.partial(dense_kernel, blocks, slots),
        out_shape=(shape, shape, jax.ShapeDtypeStruct((strips.shape[0], 2 * BL), f32)),
        in_specs=[vspec()],
        out_specs=(vspec(), vspec(), vspec()),
        scratch_shapes=[pltpu.VMEM((strips.shape[0] * slots * SUB, BL), f32)],
        compiler_params=params(),
        cost_estimate=pl.CostEstimate(flops=4 * 10**8, bytes_accessed=3 * 10**6, transcendentals=0),
        name=name,
    )(strips)


NT = (((1,), (1,)), ((), ()))
NN = (((1,), (0,)), ((), ()))


def two_planes(value):
    upper = value.astype(bf16)
    return jnp.concatenate([upper, (value - upper.astype(f32)).astype(bf16)], axis=0)


def fold(both):
    rows = both.shape[0] // 2
    return both[:rows] + both[rows:]


def twice(planes):
    return jnp.concatenate([planes, planes], axis=1)


def scores(planes, factors):
    return fold(lax.dot_general(planes, factors, NT, preferred_element_type=f32))


def combine(weighted, factors):
    return jnp.dot(two_planes(weighted), factors, preferred_element_type=f32)


def join(both):
    rank = both.shape[1] // 2
    return fold(both[:, :rank] + both[:, rank:])


def columns(ref, first, count):
    return jnp.concatenate([ref[first + k] for k in range(count)], axis=1)


def split(codes, step):
    value = codes.astype(f32) * step
    upper = value.astype(bf16)
    return upper, (value - upper.astype(f32)).astype(bf16)


def iterate(ones_ref, factors_ref, residual, start):
    rows, rank = residual.shape
    group = GROUP * BL
    steps = factors_ref.shape[0] // group

    def part(g, planes):
        factors = factors_ref[pl.ds(pl.multiple_of(g * group, group), group), :]
        score = scores(planes, factors)
        return score, columns(ones_ref, g * GROUP, GROUP) * score, factors

    def operator(direction):
        planes = twice(two_planes(direction))

        def step(g, total):
            _, weighted, factors = part(g, planes)
            return total + combine(weighted, factors)

        total = lax.fori_loop(0, steps, step, jnp.zeros((2 * rows, 2 * rank), f32))
        return join(total) + LAM * direction

    def energy(direction):
        planes = twice(two_planes(direction))

        def step(g, total):
            score, weighted, _ = part(g, planes)
            return total + jnp.sum(score * weighted, axis=-1, keepdims=True)

        total = lax.fori_loop(0, steps, step, jnp.zeros((rows, 1), f32))
        return total + LAM * jnp.sum(direction * direction, axis=-1, keepdims=True)

    solution = start
    direction = residual
    norm_now = jnp.sum(residual * residual, axis=-1, keepdims=True)
    for iteration in range(ITERS):
        if iteration + 1 == ITERS:
            return solution + norm_now / (energy(direction) + EPS) * direction
        image = operator(direction)
        alpha = norm_now / (jnp.sum(direction * image, axis=-1, keepdims=True) + EPS)
        solution = solution + alpha * direction
        residual = residual - alpha * image
        norm_next = jnp.sum(residual * residual, axis=-1, keepdims=True)
        direction = residual + norm_next / (norm_now + EPS) * direction
        norm_now = norm_next


def item_kernel(start_ref, ones_ref, right_ref, step_ref, core_ref, own_ref, other_ref, out_ref, factors_ref, total_ref):
    g = pl.program_id(0)
    sources, chips, part, rank = own_ref.shape
    per = BL // part
    group = sources * 2 * chips * part
    core = core_ref[0]

    @pl.when(g == 0)
    def _():
        total_ref[...] = jnp.zeros_like(total_ref)

    for ref, which in ((own_ref, core), (other_ref, 1 - core)):
        for z in range(chips):
            step = step_ref[pl.ds(2 * z + which, 1), :]
            for k in range(sources):
                codes = ref[k, z].astype(i32)
                start = g * group + (k // per * 2 * chips + 2 * z + which) * BL + k % per * part
                rows = pl.ds(pl.multiple_of(start, part), part)
                factors_ref[rows, :rank], factors_ref[rows, rank:] = split(codes, step)
    factors = factors_ref[pl.ds(pl.multiple_of(g * group, group), group), :]
    count = group // BL
    score = scores(twice(two_planes(start_ref[...])), factors)
    weighted = columns(right_ref, g * count, count) - columns(ones_ref, g * count, count) * score
    total_ref[...] += combine(weighted, factors)

    @pl.when(g == pl.num_programs(0) - 1)
    def _():
        start = start_ref[...]
        found = iterate(ones_ref, factors_ref, join(total_ref[...]) - LAM * start, start)
        exponent = column_exponents(jnp.max(jnp.abs(found), axis=0, keepdims=True))
        codes = fixed_point(found, power_of_two(-exponent)).astype(jnp.int16)
        exponents = jnp.broadcast_to(exponent, (16, rank)).astype(jnp.int16)[:SUB]
        for d in range(out_ref.shape[0]):
            out_ref[d, : found.shape[0], :] = codes
            out_ref[d, found.shape[0] :, :] = exponents


def gathered_spec(shape, grid):
    return pl.BlockSpec((shape[0] // grid,) + shape[1:], lambda s: (s, 0, 0, 0))


def solve_items(start, ones, right, step, core, own, other, copies):
    rows, rank = start.shape
    whole = 2 * own.size // rank
    grid = whole // (GROUP * BL)
    ones = ones.reshape(-1, rows, BL)
    right = right.reshape(-1, rows, BL)
    fixed3 = pl.BlockSpec(ones.shape, lambda s: (0, 0, 0), pipeline_mode=pl.Buffered(1))
    codes = gathered_spec(own.shape, grid)
    return pl.pallas_call(
        item_kernel,
        grid=(grid,),
        out_shape=jax.ShapeDtypeStruct((copies, rows + SUB, rank), jnp.int16),
        in_specs=[
            pl.BlockSpec((rows, rank), lambda s: (0, 0)),
            fixed3,
            fixed3,
            pl.BlockSpec(step.shape, lambda s: (0, 0)),
            pl.BlockSpec(memory_space=pltpu.SMEM),
            codes,
            codes,
        ],
        out_specs=pl.BlockSpec((copies, rows + SUB, rank), lambda s: (0, 0, 0)),
        scratch_shapes=[pltpu.VMEM((whole, 2 * rank), bf16), pltpu.VMEM((2 * rows, 2 * rank), f32)],
        compiler_params=params(),
        cost_estimate=pl.CostEstimate(flops=12 * 10**9, bytes_accessed=10**7, transcendentals=0),
        name="solve_items",
    )(start, ones, right, step, core, own, other)


def held_kernel(place_ref, ones_ref, right_ref, own_ref, other_ref, out_ref, items_ref, factors_ref):
    sources, chips, depth, rank = own_ref.shape
    part = depth - SUB
    blocks = part // SUB
    shard = blocks * BL
    group = GROUP * BL
    core = place_ref[0]

    def decode(o, carry):
        for ref, which in ((own_ref, core), (other_ref, 1 - core)):
            exponents = [ref[o, z, part:depth, :].astype(i32)[:1] for z in range(chips)]
            step = power_of_two(jnp.concatenate(exponents, axis=0))
            for z in range(0, chips, 2):
                codes = [ref[o, n, :part, :].astype(i32).astype(f32) * step[n : n + 1] for n in (z, z + 1)]
                for b in range(blocks):
                    start = o * shard + b * BL + which * (BL // 2) + z * SUB
                    rows = pl.ds(pl.multiple_of(start, 2 * SUB), 2 * SUB)
                    span = slice(b * SUB, (b + 1) * SUB)
                    value = jnp.concatenate([codes[0][span], codes[1][span]], axis=0)
                    upper = value.astype(bf16)
                    factors_ref[rows, :rank] = upper
                    factors_ref[rows, rank:] = (value - upper.astype(f32)).astype(bf16)
        return carry

    lax.fori_loop(0, sources, decode, 0, unroll=4)
    total = jnp.zeros((2 * out_ref.shape[1], 2 * rank), f32)
    for g in range(factors_ref.shape[0] // group):
        factors = factors_ref[g * group : (g + 1) * group, :]
        total = total + combine(columns(right_ref, g * GROUP, GROUP), factors)
    mine = factors_ref[pl.ds(pl.multiple_of(place_ref[1] * shard, shard), shard), :]
    items_ref[...] = mine[:, :rank].astype(f32) + mine[:, rank:].astype(f32)
    residual = join(total)
    found = iterate(ones_ref, factors_ref, residual, jnp.zeros_like(residual))
    for d in range(out_ref.shape[0]):
        out_ref[d] = found


def solve_held(place, ones, right, own, other, rows, copies):
    sources, chips, depth, rank = own.shape
    whole = 2 * sources * chips * (depth - SUB)
    shard = whole // sources
    return pl.pallas_call(
        held_kernel,
        out_shape=(jax.ShapeDtypeStruct((copies, rows, rank), f32), jax.ShapeDtypeStruct((shard, rank), f32)),
        in_specs=[pl.BlockSpec(memory_space=pltpu.SMEM), vspec(), vspec(), vspec(), vspec()],
        out_specs=(vspec(), vspec()),
        scratch_shapes=[pltpu.VMEM((whole, 2 * rank), bf16)],
        compiler_params=params(),
        name="solve_held",
    )(place, ones.reshape(-1, rows, BL), right.reshape(-1, rows, BL), own, other)


def shards(
    user_factors,
    item_factors,
    tile_user,
    tile_item,
    tile_count,
    tile_conf,
    held_user,
    held_item,
    held_count,
    held_conf,
):
    rank = user_factors.shape[1]
    chips = lax.axis_size("z")
    core = lax.axis_index("c")
    chip = lax.axis_index("z")
    me = lax.axis_index(USER)
    column = lax.axis_index(ITEM)
    peers, item_peers = lax.axis_size(USER), lax.axis_size(ITEM)
    slots = tile_user.shape[-1]
    held_slots = held_user.shape[-1]
    user_blocks = user_factors.shape[0] // BL
    item_blocks = item_factors.shape[0] // BL
    held_blocks = 2
    siblings = [(0, 1), (1, 0)]

    part = user_factors.shape[0] // item_peers
    piece, exponent = pack_users(user_factors, column, chips, part)
    piece = lax.all_to_all(piece, "z", 0, 0, tiled=True)

    blocks = peers * user_blocks * item_blocks
    order = [c * chips + z for z in range(chips) for c in range(2)]
    strips = cut_strips(
        me, tile_user[0, 0].T, tile_item[0, 0].T, tile_count[0, 0], tile_conf, exponent,
        True, order, (peers, 1), item_blocks, blocks, "cut_items",
    )
    held_all = item_peers * item_blocks * held_blocks
    held_strips = cut_strips(
        column, held_item[0, 0].T, held_user[0, 0].T, held_count[0, 0], held_conf, jnp.zeros_like(exponent),
        False, list(range(item_peers)), (1, item_blocks), held_blocks, held_all, "cut_held",
    )
    strips, held_strips, piece = lax.optimization_barrier((strips, held_strips, piece))
    strips = lax.all_to_all(strips, USER, 0, 0, tiled=True)
    own_users = lax.all_gather(piece, ITEM, axis=0, tiled=False)
    strips, own_users, held_strips = lax.optimization_barrier((strips, own_users, held_strips))
    other_users = lax.ppermute(own_users, "c", siblings)
    held_strips = lax.all_to_all(held_strips, ITEM, 0, 0, tiled=True)
    ones, right, step = dense(strips, blocks, peers * slots, "dense_items")

    start = lax.dynamic_slice_in_dim(
        item_factors.reshape(item_blocks, peers, SUB, rank), core * chips + chip, 1, axis=1
    ).reshape(item_blocks * SUB, rank)
    mine = solve_items(start, ones, right, step, core.reshape(1), own_users, other_users, chips)
    mine, held_strips = lax.optimization_barrier((mine, held_strips))
    held_ones, held_right, _ = dense(held_strips, held_all, item_peers * held_slots, "dense_held")

    mine = lax.all_to_all(mine, "z", 0, 0, tiled=True)
    own = lax.all_gather(mine, ITEM, axis=0, tiled=False)
    other = lax.ppermute(own, "c", siblings)
    folded, new_items = solve_held(
        jnp.stack([core, column]), held_ones, held_right, own, other, held_blocks * SUB, item_peers
    )
    folded = lax.all_to_all(folded, ITEM, 0, 0, tiled=True)
    folded = folded.reshape(item_peers, held_blocks, SUB, rank).transpose(1, 0, 2, 3).reshape(-1, rank)
    return new_items, folded


def solution(mesh):
    split = jax.sharding.Mesh(mesh.devices.reshape(mesh.shape["user"] // 2, 2, -1, 4), ("z", "c", "y", "x"))
    in_specs = (
        P(USER, None),
        P(ITEM, None),
        P(ITEM, USER, None, None),
        P(ITEM, USER, None, None),
        P(ITEM, USER, None),
        P(ITEM, USER, None, None, None, None),
        P(USER, ITEM, None, None),
        P(USER, ITEM, None, None),
        P(USER, ITEM, None),
        P(USER, ITEM, None, None, None, None),
    )
    out_specs = (P(ITEM, None), P(USER, None))
    return jax.shard_map(shards, mesh=split, in_specs=in_specs, out_specs=out_specs, check_vma=False)
```

```python
import functools

import jax
import jax.numpy as jnp
from jax import lax
from jax.experimental import pallas as pl
from jax.experimental.pallas import tpu as pltpu
from jax.sharding import PartitionSpec as P

ITERS = 2
LAM = 1.0
EPS = 1e-6
BL = 128
SUB = 8
GROUP = 32
USER = ("z", "c")
ITEM = ("y", "x")
VMEM = 28 * 1024 * 1024

i32 = jnp.int32
f32 = jnp.float32
bf16 = jnp.bfloat16


def params():
    return pltpu.CompilerParams(vmem_limit_bytes=VMEM)


def vspec():
    return pl.BlockSpec(memory_space=pltpu.VMEM)


def power_of_two(exponent):
    bits = exponent + 126
    value = jnp.full(exponent.shape, 2.0**-126, f32)
    for k, power in enumerate((1, 2, 4, 8, 16, 32, 64)):
        value = value * jnp.where((bits >> k) & 1 == 1, f32(2.0**power), f32(1.0))
    high = jnp.where(bits >= 128, f32(2.0**64), f32(1.0))
    return value * high * high


def column_exponents(peak):
    rest = jnp.clip(peak, 2.0**-45, 2.0**60) * f32(2.0**60)
    found = jnp.zeros(peak.shape, i32)
    for k in (64, 32, 16, 8, 4, 2, 1):
        big = rest >= f32(2.0**k)
        rest = jnp.where(big, rest * f32(2.0**-k), rest)
        found = found + jnp.where(big, k, 0)
    return found - 74


def fixed_point(rows, inverse_step):
    return jnp.clip(jnp.round(rows * inverse_step), -32767.0, 32767.0).astype(i32)


def pack_users_kernel(place_ref, rows_ref, out_ref, exponent_ref):
    exponent = column_exponents(jnp.max(jnp.abs(rows_ref[...]), axis=0, keepdims=True))
    peers, part, rank = out_ref.shape
    first = pl.multiple_of(place_ref[0] * part, part)
    codes = fixed_point(rows_ref[pl.ds(first, part), :], power_of_two(-exponent)).astype(jnp.int16)
    for z in range(peers):
        out_ref[z] = codes
    exponent_ref[...] = exponent.astype(f32)


def pack_users(rows, place, peers, part):
    rank = rows.shape[1]
    return pl.pallas_call(
        pack_users_kernel,
        out_shape=(jax.ShapeDtypeStruct((peers, part, rank), jnp.int16), jax.ShapeDtypeStruct((1, rank), f32)),
        in_specs=[pl.BlockSpec(memory_space=pltpu.SMEM), vspec()],
        out_specs=(vspec(), vspec()),
        name="pack_users",
    )(place.reshape(1), rows)


def strips_kernel(turn, order, owner_scale, slot_scale, dead, place_ref, outer_ref, inner_ref, count_ref, tiles_ref, extra_ref, out_ref):
    slots, owners = outer_ref.shape
    total = owners * slots
    for t in range(0, total, 2):
        pair = [tiles_ref[t + k].astype(f32) for k in range(2)]
        if turn:
            pair = [tile.T for tile in pair]
        for d in range(len(order)):
            q = order[d] * SUB
            both = jnp.concatenate([pair[0][q : q + SUB], pair[1][q : q + SUB]], axis=0)
            out_ref[d, t * SUB : (t + 2) * SUB, :] = both.astype(bf16)
    outer_scale, owner_scale = owner_scale
    per = BL // total
    row = lax.broadcasted_iota(i32, (16, BL), 0)
    lane = lax.broadcasted_iota(i32, (16, BL), 1)
    place = place_ref[0]
    mine = jnp.where(row == place // per, lane - lax.rem(place, per) * total, -1)
    codes = jnp.zeros((16, BL), f32)
    for o in range(owners):
        for c in range(slots):
            code = (outer_ref[c, o] * outer_scale + o * owner_scale) * slot_scale + inner_ref[c, o]
            code = jnp.where(c < count_ref[o], code, dead)
            codes = jnp.where(mine == o * slots + c, code.astype(f32), codes)
    below = owners * total // BL
    for k in range(extra_ref.shape[1] // BL):
        codes = jnp.where(row == below + k, extra_ref[:, k * BL : (k + 1) * BL], codes)
    codes = codes.astype(bf16)
    for d in range(len(order)):
        out_ref[d, total * SUB :, :] = codes


def cut_strips(place, outer, inner, count, tiles, extra, turn, order, owner_scale, slot_scale, dead, name):
    slots, owners = outer.shape
    smem = pl.BlockSpec(memory_space=pltpu.SMEM)
    return pl.pallas_call(
        functools.partial(strips_kernel, turn, order, owner_scale, slot_scale, dead),
        out_shape=jax.ShapeDtypeStruct((len(order), owners * slots * SUB + 16, BL), bf16),
        in_specs=[smem, smem, smem, smem, vspec(), vspec()],
        out_specs=vspec(),
        compiler_params=params(),
        cost_estimate=pl.CostEstimate(flops=10**6, bytes_accessed=2 * 10**6, transcendentals=0),
        name=name,
    )(place.reshape(1), outer, inner, count, tiles.reshape(-1, BL, BL), extra)


def dense_kernel(blocks, slots, strips_ref, ones_ref, right_ref, step_ref, wide_ref):
    sources, depth, _ = strips_ref.shape
    count = slots * SUB
    table = strips_ref[0, count:depth, :].astype(f32)
    for s in range(1, sources):
        table = table + strips_ref[s, count:depth, :].astype(f32)
    held = sources * slots // BL
    codes = jnp.concatenate([table[k : k + 1, :] for k in range(held)], axis=1).astype(i32)
    rows = [strips_ref[s, count:depth, :].astype(f32) for s in range(sources)]
    rows = [jnp.concatenate([row[held : held + 1], row[held + 1 : held + 2]], axis=1) for row in rows]
    step_ref[...] = power_of_two(jnp.concatenate(rows, axis=0).astype(i32))
    named = lax.broadcasted_iota(i32, (blocks, sources * slots), 0) == codes
    named = jnp.where(named, f32(1.0), f32(0.0))
    live = jnp.sum(named, axis=1, keepdims=True)
    named = named.astype(bf16)
    for s in range(sources):
        wide_ref[s * count : (s + 1) * count, :] = strips_ref[s, :count, :].astype(f32)
    for r in range(0, SUB, 2):
        rows = [wide_ref[pl.ds(r + k, sources * slots, stride=SUB), :].astype(bf16) for k in range(2)]
        both = jnp.dot(named, jnp.concatenate(rows, axis=1), preferred_element_type=f32)
        for k in range(2):
            total = both[:, k * BL : (k + 1) * BL]
            ones_ref[pl.ds(r + k, blocks, stride=SUB), :] = total + 1.0
            right_ref[pl.ds(r + k, blocks, stride=SUB), :] = total + live


def dense(strips, blocks, slots, name):
    shape = jax.ShapeDtypeStruct((blocks * SUB, BL), f32)
    return pl.pallas_call(
        functools.partial(dense_kernel, blocks, slots),
        out_shape=(shape, shape, jax.ShapeDtypeStruct((strips.shape[0], 2 * BL), f32)),
        in_specs=[vspec()],
        out_specs=(vspec(), vspec(), vspec()),
        scratch_shapes=[pltpu.VMEM((strips.shape[0] * slots * SUB, BL), f32)],
        compiler_params=params(),
        cost_estimate=pl.CostEstimate(flops=4 * 10**8, bytes_accessed=3 * 10**6, transcendentals=0),
        name=name,
    )(strips)


NT = (((1,), (1,)), ((), ()))
NN = (((1,), (0,)), ((), ()))


def two_planes(value):
    upper = value.astype(bf16)
    return jnp.concatenate([upper, (value - upper.astype(f32)).astype(bf16)], axis=0)


def fold(both):
    rows = both.shape[0] // 2
    return both[:rows] + both[rows:]


def twice(planes):
    return jnp.concatenate([planes, planes], axis=1)


def scores(planes, factors):
    return fold(lax.dot_general(planes, factors, NT, preferred_element_type=f32))


def combine(weighted, factors):
    return jnp.dot(two_planes(weighted), factors, preferred_element_type=f32)


def join(both):
    rank = both.shape[1] // 2
    return fold(both[:, :rank] + both[:, rank:])


def columns(ref, first, count):
    return jnp.concatenate([ref[first + k] for k in range(count)], axis=1)


def split(codes, step):
    value = codes.astype(f32) * step
    upper = value.astype(bf16)
    return upper, (value - upper.astype(f32)).astype(bf16)


def iterate(ones_ref, factors_ref, residual, start):
    rows, rank = residual.shape
    group = GROUP * BL
    steps = factors_ref.shape[0] // group

    def operator(direction):
        planes = twice(two_planes(direction))

        def step(g, total):
            factors = factors_ref[pl.ds(pl.multiple_of(g * group, group), group), :]
            weighted = columns(ones_ref, g * GROUP, GROUP) * scores(planes, factors)
            return total + combine(weighted, factors)

        total = lax.fori_loop(0, steps, step, jnp.zeros((2 * rows, 2 * rank), f32))
        return join(total) + LAM * direction

    def energy(direction):
        score = scores(twice(two_planes(direction)), factors_ref[...])
        weighted = columns(ones_ref, 0, factors_ref.shape[0] // BL) * score
        return jnp.sum(score * weighted, axis=-1, keepdims=True) + LAM * jnp.sum(
            direction * direction, axis=-1, keepdims=True
        )

    solution = start
    direction = residual
    norm_now = jnp.sum(residual * residual, axis=-1, keepdims=True)
    for iteration in range(ITERS):
        if iteration + 1 == ITERS:
            return solution + norm_now / (energy(direction) + EPS) * direction
        image = operator(direction)
        alpha = norm_now / (jnp.sum(direction * image, axis=-1, keepdims=True) + EPS)
        solution = solution + alpha * direction
        residual = residual - alpha * image
        norm_next = jnp.sum(residual * residual, axis=-1, keepdims=True)
        direction = residual + norm_next / (norm_now + EPS) * direction
        norm_now = norm_next


def item_kernel(start_ref, ones_ref, right_ref, step_ref, core_ref, own_ref, other_ref, out_ref, factors_ref, total_ref):
    g = pl.program_id(0)
    sources, chips, part, rank = own_ref.shape
    per = BL // part
    group = sources * 2 * chips * part
    core = core_ref[0]

    @pl.when(g == 0)
    def _():
        total_ref[...] = jnp.zeros_like(total_ref)

    for ref, which in ((own_ref, core), (other_ref, 1 - core)):
        for z in range(chips):
            step = step_ref[pl.ds(2 * z + which, 1), :]
            for k in range(sources):
                codes = ref[k, z].astype(i32)
                start = g * group + (k // per * 2 * chips + 2 * z + which) * BL + k % per * part
                rows = pl.ds(pl.multiple_of(start, part), part)
                factors_ref[rows, :rank], factors_ref[rows, rank:] = split(codes, step)
    factors = factors_ref[pl.ds(pl.multiple_of(g * group, group), group), :]
    count = group // BL
    score = scores(twice(two_planes(start_ref[...])), factors)
    weighted = columns(right_ref, g * count, count) - columns(ones_ref, g * count, count) * score
    total_ref[...] += combine(weighted, factors)

    @pl.when(g == pl.num_programs(0) - 1)
    def _():
        start = start_ref[...]
        found = iterate(ones_ref, factors_ref, join(total_ref[...]) - LAM * start, start)
        exponent = column_exponents(jnp.max(jnp.abs(found), axis=0, keepdims=True))
        codes = fixed_point(found, power_of_two(-exponent)).astype(jnp.int16)
        exponents = jnp.broadcast_to(exponent, (16, rank)).astype(jnp.int16)[:SUB]
        for d in range(out_ref.shape[0]):
            out_ref[d, : found.shape[0], :] = codes
            out_ref[d, found.shape[0] :, :] = exponents


def gathered_spec(shape, grid):
    return pl.BlockSpec((shape[0] // grid,) + shape[1:], lambda s: (s, 0, 0, 0))


def solve_items(start, ones, right, step, core, own, other, copies):
    rows, rank = start.shape
    whole = 2 * own.size // rank
    grid = whole // (GROUP * BL)
    ones = ones.reshape(-1, rows, BL)
    right = right.reshape(-1, rows, BL)
    fixed3 = pl.BlockSpec(ones.shape, lambda s: (0, 0, 0), pipeline_mode=pl.Buffered(1))
    codes = gathered_spec(own.shape, grid)
    return pl.pallas_call(
        item_kernel,
        grid=(grid,),
        out_shape=jax.ShapeDtypeStruct((copies, rows + SUB, rank), jnp.int16),
        in_specs=[
            pl.BlockSpec((rows, rank), lambda s: (0, 0)),
            fixed3,
            fixed3,
            pl.BlockSpec(step.shape, lambda s: (0, 0)),
            pl.BlockSpec(memory_space=pltpu.SMEM),
            codes,
            codes,
        ],
        out_specs=pl.BlockSpec((copies, rows + SUB, rank), lambda s: (0, 0, 0)),
        scratch_shapes=[pltpu.VMEM((whole, 2 * rank), bf16), pltpu.VMEM((2 * rows, 2 * rank), f32)],
        compiler_params=params(),
        cost_estimate=pl.CostEstimate(flops=12 * 10**9, bytes_accessed=10**7, transcendentals=0),
        name="solve_items",
    )(start, ones, right, step, core, own, other)


def held_kernel(place_ref, ones_ref, right_ref, own_ref, other_ref, out_ref, items_ref, factors_ref):
    sources, chips, depth, rank = own_ref.shape
    part = depth - SUB
    blocks = part // SUB
    shard = blocks * BL
    group = GROUP * BL
    core = place_ref[0]

    def decode(o, carry):
        for ref, which in ((own_ref, core), (other_ref, 1 - core)):
            exponents = [ref[o, z, part:depth, :].astype(i32)[:1] for z in range(chips)]
            step = power_of_two(jnp.concatenate(exponents, axis=0))
            for z in range(0, chips, 2):
                codes = [ref[o, n, :part, :].astype(i32).astype(f32) * step[n : n + 1] for n in (z, z + 1)]
                for b in range(blocks):
                    start = o * shard + b * BL + which * (BL // 2) + z * SUB
                    rows = pl.ds(pl.multiple_of(start, 2 * SUB), 2 * SUB)
                    span = slice(b * SUB, (b + 1) * SUB)
                    value = jnp.concatenate([codes[0][span], codes[1][span]], axis=0)
                    upper = value.astype(bf16)
                    factors_ref[rows, :rank] = upper
                    factors_ref[rows, rank:] = (value - upper.astype(f32)).astype(bf16)
        return carry

    lax.fori_loop(0, sources, decode, 0, unroll=4)
    total = jnp.zeros((2 * out_ref.shape[1], 2 * rank), f32)
    for g in range(factors_ref.shape[0] // group):
        factors = factors_ref[g * group : (g + 1) * group, :]
        total = total + combine(columns(right_ref, g * GROUP, GROUP), factors)
    mine = factors_ref[pl.ds(pl.multiple_of(place_ref[1] * shard, shard), shard), :]
    items_ref[...] = mine[:, :rank].astype(f32) + mine[:, rank:].astype(f32)
    residual = join(total)
    found = iterate(ones_ref, factors_ref, residual, jnp.zeros_like(residual))
    for d in range(out_ref.shape[0]):
        out_ref[d] = found


def solve_held(place, ones, right, own, other, rows, copies):
    sources, chips, depth, rank = own.shape
    whole = 2 * sources * chips * (depth - SUB)
    shard = whole // sources
    return pl.pallas_call(
        held_kernel,
        out_shape=(jax.ShapeDtypeStruct((copies, rows, rank), f32), jax.ShapeDtypeStruct((shard, rank), f32)),
        in_specs=[pl.BlockSpec(memory_space=pltpu.SMEM), vspec(), vspec(), vspec(), vspec()],
        out_specs=(vspec(), vspec()),
        scratch_shapes=[pltpu.VMEM((whole, 2 * rank), bf16)],
        compiler_params=params(),
        name="solve_held",
    )(place, ones.reshape(-1, rows, BL), right.reshape(-1, rows, BL), own, other)


def shards(
    user_factors,
    item_factors,
    tile_user,
    tile_item,
    tile_count,
    tile_conf,
    held_user,
    held_item,
    held_count,
    held_conf,
):
    rank = user_factors.shape[1]
    chips = lax.axis_size("z")
    core = lax.axis_index("c")
    chip = lax.axis_index("z")
    me = lax.axis_index(USER)
    column = lax.axis_index(ITEM)
    peers, item_peers = lax.axis_size(USER), lax.axis_size(ITEM)
    slots = tile_user.shape[-1]
    held_slots = held_user.shape[-1]
    user_blocks = user_factors.shape[0] // BL
    item_blocks = item_factors.shape[0] // BL
    held_blocks = 2
    siblings = [(0, 1), (1, 0)]

    part = user_factors.shape[0] // item_peers
    piece, exponent = pack_users(user_factors, column, chips, part)
    piece = lax.all_to_all(piece, "z", 0, 0, tiled=True)

    blocks = peers * user_blocks * item_blocks
    order = [c * chips + z for z in range(chips) for c in range(2)]
    strips = cut_strips(
        me, tile_user[0, 0].T, tile_item[0, 0].T, tile_count[0, 0], tile_conf, exponent,
        True, order, (peers, 1), item_blocks, blocks, "cut_items",
    )
    held_all = item_peers * item_blocks * held_blocks
    held_strips = cut_strips(
        column, held_item[0, 0].T, held_user[0, 0].T, held_count[0, 0], held_conf, jnp.zeros_like(exponent),
        False, list(range(item_peers)), (1, item_blocks), held_blocks, held_all, "cut_held",
    )
    strips, held_strips, piece = lax.optimization_barrier((strips, held_strips, piece))
    strips = lax.all_to_all(strips, USER, 0, 0, tiled=True)
    own_users = lax.all_gather(piece, ITEM, axis=0, tiled=False)
    strips, own_users, held_strips = lax.optimization_barrier((strips, own_users, held_strips))
    other_users = lax.ppermute(own_users, "c", siblings)
    held_strips = lax.all_to_all(held_strips, ITEM, 0, 0, tiled=True)
    ones, right, step = dense(strips, blocks, peers * slots, "dense_items")

    start = lax.dynamic_slice_in_dim(
        item_factors.reshape(item_blocks, peers, SUB, rank), core * chips + chip, 1, axis=1
    ).reshape(item_blocks * SUB, rank)
    mine = solve_items(start, ones, right, step, core.reshape(1), own_users, other_users, chips)
    mine, held_strips = lax.optimization_barrier((mine, held_strips))
    held_ones, held_right, _ = dense(held_strips, held_all, item_peers * held_slots, "dense_held")

    mine = lax.all_to_all(mine, "z", 0, 0, tiled=True)
    own = lax.all_gather(mine, ITEM, axis=0, tiled=False)
    other = lax.ppermute(own, "c", siblings)
    folded, new_items = solve_held(
        jnp.stack([core, column]), held_ones, held_right, own, other, held_blocks * SUB, item_peers
    )
    folded = lax.all_to_all(folded, ITEM, 0, 0, tiled=True)
    folded = folded.reshape(item_peers, held_blocks, SUB, rank).transpose(1, 0, 2, 3).reshape(-1, rank)
    return new_items, folded


def solution(mesh):
    split = jax.sharding.Mesh(mesh.devices.reshape(mesh.shape["user"] // 2, 2, -1, 4), ("z", "c", "y", "x"))
    in_specs = (
        P(USER, None),
        P(ITEM, None),
        P(ITEM, USER, None, None),
        P(ITEM, USER, None, None),
        P(ITEM, USER, None),
        P(ITEM, USER, None, None, None, None),
        P(USER, ITEM, None, None),
        P(USER, ITEM, None, None),
        P(USER, ITEM, None),
        P(USER, ITEM, None, None, None, None),
    )
    out_specs = (P(ITEM, None), P(USER, None))
    return jax.shard_map(shards, mesh=split, in_specs=in_specs, out_specs=out_specs, check_vma=False)
```

```python
import functools

import jax
import jax.numpy as jnp
from jax import lax
from jax.experimental import pallas as pl
from jax.experimental.pallas import tpu as pltpu
from jax.sharding import PartitionSpec as P

ITERS = 2
LAM = 1.0
EPS = 1e-6
BL = 128
SUB = 8
GROUP = 32
USER = ("z", "c")
ITEM = ("y", "x")
VMEM = 28 * 1024 * 1024

i32 = jnp.int32
f32 = jnp.float32
bf16 = jnp.bfloat16


def params():
    return pltpu.CompilerParams(vmem_limit_bytes=VMEM)


def vspec():
    return pl.BlockSpec(memory_space=pltpu.VMEM)


def power_of_two(exponent):
    bits = exponent + 126
    value = jnp.full(exponent.shape, 2.0**-126, f32)
    for k, power in enumerate((1, 2, 4, 8, 16, 32, 64)):
        value = value * jnp.where((bits >> k) & 1 == 1, f32(2.0**power), f32(1.0))
    high = jnp.where(bits >= 128, f32(2.0**64), f32(1.0))
    return value * high * high


def column_exponents(peak):
    rest = jnp.clip(peak, 2.0**-45, 2.0**60) * f32(2.0**60)
    found = jnp.zeros(peak.shape, i32)
    for k in (64, 32, 16, 8, 4, 2, 1):
        big = rest >= f32(2.0**k)
        rest = jnp.where(big, rest * f32(2.0**-k), rest)
        found = found + jnp.where(big, k, 0)
    return found - 74


def fixed_point(rows, inverse_step):
    return jnp.clip(jnp.round(rows * inverse_step), -32767.0, 32767.0).astype(i32)


def pack_users_kernel(place_ref, rows_ref, out_ref, exponent_ref):
    exponent = column_exponents(jnp.max(jnp.abs(rows_ref[...]), axis=0, keepdims=True))
    peers, part, rank = out_ref.shape
    first = pl.multiple_of(place_ref[0] * part, part)
    codes = fixed_point(rows_ref[pl.ds(first, part), :], power_of_two(-exponent)).astype(jnp.int16)
    for z in range(peers):
        out_ref[z] = codes
    exponent_ref[...] = exponent.astype(f32)


def pack_users(rows, place, peers, part):
    rank = rows.shape[1]
    return pl.pallas_call(
        pack_users_kernel,
        out_shape=(jax.ShapeDtypeStruct((peers, part, rank), jnp.int16), jax.ShapeDtypeStruct((1, rank), f32)),
        in_specs=[pl.BlockSpec(memory_space=pltpu.SMEM), vspec()],
        out_specs=(vspec(), vspec()),
        name="pack_users",
    )(place.reshape(1), rows)


def strips_kernel(turn, order, owner_scale, slot_scale, dead, place_ref, outer_ref, inner_ref, count_ref, tiles_ref, extra_ref, out_ref):
    slots, owners = outer_ref.shape
    total = owners * slots
    for t in range(0, total, 2):
        pair = [tiles_ref[t + k].astype(f32) for k in range(2)]
        if turn:
            pair = [tile.T for tile in pair]
        for d in range(len(order)):
            q = order[d] * SUB
            both = jnp.concatenate([pair[0][q : q + SUB], pair[1][q : q + SUB]], axis=0)
            out_ref[d, t * SUB : (t + 2) * SUB, :] = both.astype(bf16)
    outer_scale, owner_scale = owner_scale
    per = BL // total
    row = lax.broadcasted_iota(i32, (16, BL), 0)
    lane = lax.broadcasted_iota(i32, (16, BL), 1)
    place = place_ref[0]
    mine = jnp.where(row == place // per, lane - lax.rem(place, per) * total, -1)
    codes = jnp.zeros((16, BL), f32)
    for o in range(owners):
        for c in range(slots):
            code = (outer_ref[c, o] * outer_scale + o * owner_scale) * slot_scale + inner_ref[c, o]
            code = jnp.where(c < count_ref[o], code, dead)
            codes = jnp.where(mine == o * slots + c, code.astype(f32), codes)
    below = owners * total // BL
    for k in range(extra_ref.shape[1] // BL):
        codes = jnp.where(row == below + k, extra_ref[:, k * BL : (k + 1) * BL], codes)
    codes = codes.astype(bf16)
    for d in range(len(order)):
        out_ref[d, total * SUB :, :] = codes


def cut_strips(place, outer, inner, count, tiles, extra, turn, order, owner_scale, slot_scale, dead, name):
    slots, owners = outer.shape
    smem = pl.BlockSpec(memory_space=pltpu.SMEM)
    return pl.pallas_call(
        functools.partial(strips_kernel, turn, order, owner_scale, slot_scale, dead),
        out_shape=jax.ShapeDtypeStruct((len(order), owners * slots * SUB + 16, BL), bf16),
        in_specs=[smem, smem, smem, smem, vspec(), vspec()],
        out_specs=vspec(),
        compiler_params=params(),
        cost_estimate=pl.CostEstimate(flops=10**6, bytes_accessed=2 * 10**6, transcendentals=0),
        name=name,
    )(place.reshape(1), outer, inner, count, tiles.reshape(-1, BL, BL), extra)


def dense_kernel(blocks, slots, strips_ref, ones_ref, right_ref, step_ref, wide_ref):
    sources, depth, _ = strips_ref.shape
    count = slots * SUB
    table = strips_ref[0, count:depth, :].astype(f32)
    for s in range(1, sources):
        table = table + strips_ref[s, count:depth, :].astype(f32)
    held = sources * slots // BL
    codes = jnp.concatenate([table[k : k + 1, :] for k in range(held)], axis=1).astype(i32)
    rows = [strips_ref[s, count:depth, :].astype(f32) for s in range(sources)]
    rows = [jnp.concatenate([row[held : held + 1], row[held + 1 : held + 2]], axis=1) for row in rows]
    step_ref[...] = power_of_two(jnp.concatenate(rows, axis=0).astype(i32))
    named = lax.broadcasted_iota(i32, (blocks, sources * slots), 0) == codes
    named = jnp.where(named, f32(1.0), f32(0.0))
    live = jnp.sum(named, axis=1, keepdims=True)
    named = named.astype(bf16)
    for s in range(sources):
        wide_ref[s * count : (s + 1) * count, :] = strips_ref[s, :count, :].astype(f32)
    for r in range(0, SUB, 2):
        rows = [wide_ref[pl.ds(r + k, sources * slots, stride=SUB), :].astype(bf16) for k in range(2)]
        both = jnp.dot(named, jnp.concatenate(rows, axis=1), preferred_element_type=f32)
        for k in range(2):
            total = both[:, k * BL : (k + 1) * BL]
            ones_ref[pl.ds(r + k, blocks, stride=SUB), :] = total + 1.0
            right_ref[pl.ds(r + k, blocks, stride=SUB), :] = total + live


def dense(strips, blocks, slots, name):
    shape = jax.ShapeDtypeStruct((blocks * SUB, BL), f32)
    return pl.pallas_call(
        functools.partial(dense_kernel, blocks, slots),
        out_shape=(shape, shape, jax.ShapeDtypeStruct((strips.shape[0], 2 * BL), f32)),
        in_specs=[vspec()],
        out_specs=(vspec(), vspec(), vspec()),
        scratch_shapes=[pltpu.VMEM((strips.shape[0] * slots * SUB, BL), f32)],
        compiler_params=params(),
        cost_estimate=pl.CostEstimate(flops=4 * 10**8, bytes_accessed=3 * 10**6, transcendentals=0),
        name=name,
    )(strips)


NT = (((1,), (1,)), ((), ()))
NN = (((1,), (0,)), ((), ()))


def two_planes(value):
    upper = value.astype(bf16)
    return jnp.concatenate([upper, (value - upper.astype(f32)).astype(bf16)], axis=0)


def fold(both):
    rows = both.shape[0] // 2
    return both[:rows] + both[rows:]


def twice(planes):
    return jnp.concatenate([planes, planes], axis=1)


def scores(planes, factors):
    return fold(lax.dot_general(planes, factors, NT, preferred_element_type=f32))


def combine(weighted, factors):
    return jnp.dot(two_planes(weighted), factors, preferred_element_type=f32)


def join(both):
    rank = both.shape[1] // 2
    return fold(both[:, :rank] + both[:, rank:])


def columns(ref, first, count, rows):
    spans = [pl.ds(pl.multiple_of((first + k) * rows, rows), rows) for k in range(count)]
    return jnp.concatenate([ref[span, :] for span in spans], axis=1)


def split(codes, step):
    value = codes.astype(f32) * step
    upper = value.astype(bf16)
    return upper, (value - upper.astype(f32)).astype(bf16)


def iterate(ones_ref, factors_ref, residual, start):
    rows, rank = residual.shape
    group = GROUP * BL
    steps = factors_ref.shape[0] // group

    def operator(direction):
        planes = twice(two_planes(direction))

        def step(g, total):
            factors = factors_ref[pl.ds(pl.multiple_of(g * group, group), group), :]
            weighted = columns(ones_ref, g * GROUP, GROUP, rows) * scores(planes, factors)
            return total + combine(weighted, factors)

        total = lax.fori_loop(0, steps, step, jnp.zeros((2 * rows, 2 * rank), f32))
        return join(total) + LAM * direction

    def energy(direction):
        score = scores(twice(two_planes(direction)), factors_ref[...])
        weighted = columns(ones_ref, 0, factors_ref.shape[0] // BL, rows) * score
        return jnp.sum(score * weighted, axis=-1, keepdims=True) + LAM * jnp.sum(
            direction * direction, axis=-1, keepdims=True
        )

    solution = start
    direction = residual
    norm_now = jnp.sum(residual * residual, axis=-1, keepdims=True)
    for iteration in range(ITERS):
        if iteration + 1 == ITERS:
            return solution + norm_now / (energy(direction) + EPS) * direction
        image = operator(direction)
        alpha = norm_now / (jnp.sum(direction * image, axis=-1, keepdims=True) + EPS)
        solution = solution + alpha * direction
        residual = residual - alpha * image
        norm_next = jnp.sum(residual * residual, axis=-1, keepdims=True)
        direction = residual + norm_next / (norm_now + EPS) * direction
        norm_now = norm_next


def item_kernel(
    slots, start_ref, strips_ref, core_ref, own_ref, other_ref, out_ref,
    factors_ref, total_ref, ones_ref, right_ref, step_ref, wide_ref,
):
    g = pl.program_id(0)
    held = start_ref.shape[0]
    sources, chips, part, rank = own_ref.shape
    per = BL // part
    group = sources * 2 * chips * part
    core = core_ref[0]

    @pl.when(g == 0)
    def _():
        total_ref[...] = jnp.zeros_like(total_ref)
        dense_kernel(ones_ref.shape[0] // SUB, slots, strips_ref, ones_ref, right_ref, step_ref, wide_ref)

    for ref, which in ((own_ref, core), (other_ref, 1 - core)):
        for z in range(chips):
            step = step_ref[pl.ds(2 * z + which, 1), :]
            for k in range(sources):
                codes = ref[k, z].astype(i32)
                start = g * group + (k // per * 2 * chips + 2 * z + which) * BL + k % per * part
                rows = pl.ds(pl.multiple_of(start, part), part)
                factors_ref[rows, :rank], factors_ref[rows, rank:] = split(codes, step)
    factors = factors_ref[pl.ds(pl.multiple_of(g * group, group), group), :]
    count = group // BL
    score = scores(twice(two_planes(start_ref[...])), factors)
    weighted = columns(right_ref, g * count, count, held) - columns(ones_ref, g * count, count, held) * score
    total_ref[...] += combine(weighted, factors)

    @pl.when(g == pl.num_programs(0) - 1)
    def _():
        start = start_ref[...]
        found = iterate(ones_ref, factors_ref, join(total_ref[...]) - LAM * start, start)
        exponent = column_exponents(jnp.max(jnp.abs(found), axis=0, keepdims=True))
        codes = fixed_point(found, power_of_two(-exponent)).astype(jnp.int16)
        exponents = jnp.broadcast_to(exponent, (16, rank)).astype(jnp.int16)[:SUB]
        for d in range(out_ref.shape[0]):
            out_ref[d, : found.shape[0], :] = codes
            out_ref[d, found.shape[0] :, :] = exponents


def gathered_spec(shape, grid):
    return pl.BlockSpec((shape[0] // grid,) + shape[1:], lambda s: (s, 0, 0, 0))


def solve_items(start, strips, slots, core, own, other, copies):
    rows, rank = start.shape
    whole = 2 * own.size // rank
    grid = whole // (GROUP * BL)
    dense_shape = (whole // BL * rows, BL)
    codes = gathered_spec(own.shape, grid)
    return pl.pallas_call(
        functools.partial(item_kernel, slots),
        grid=(grid,),
        out_shape=jax.ShapeDtypeStruct((copies, rows + SUB, rank), jnp.int16),
        in_specs=[
            pl.BlockSpec((rows, rank), lambda s: (0, 0)),
            pl.BlockSpec(strips.shape, lambda s: (0, 0, 0), pipeline_mode=pl.Buffered(1)),
            pl.BlockSpec(memory_space=pltpu.SMEM),
            codes,
            codes,
        ],
        out_specs=pl.BlockSpec((copies, rows + SUB, rank), lambda s: (0, 0, 0)),
        scratch_shapes=[
            pltpu.VMEM((whole, 2 * rank), bf16),
            pltpu.VMEM((2 * rows, 2 * rank), f32),
            pltpu.VMEM(dense_shape, f32),
            pltpu.VMEM(dense_shape, f32),
            pltpu.VMEM((strips.shape[0], 2 * BL), f32),
            pltpu.VMEM((strips.shape[0] * slots * SUB, BL), f32),
        ],
        compiler_params=params(),
        cost_estimate=pl.CostEstimate(flops=12 * 10**9, bytes_accessed=10**7, transcendentals=0),
        name="solve_items",
    )(start, strips, core, own, other)


def held_kernel(place_ref, ones_ref, right_ref, own_ref, other_ref, out_ref, items_ref, factors_ref):
    sources, chips, depth, rank = own_ref.shape
    part = depth - SUB
    blocks = part // SUB
    shard = blocks * BL
    group = GROUP * BL
    core = place_ref[0]

    def decode(o, carry):
        for ref, which in ((own_ref, core), (other_ref, 1 - core)):
            exponents = [ref[o, z, part:depth, :].astype(i32)[:1] for z in range(chips)]
            step = power_of_two(jnp.concatenate(exponents, axis=0))
            for z in range(0, chips, 2):
                codes = [ref[o, n, :part, :].astype(i32).astype(f32) * step[n : n + 1] for n in (z, z + 1)]
                for b in range(blocks):
                    start = o * shard + b * BL + which * (BL // 2) + z * SUB
                    rows = pl.ds(pl.multiple_of(start, 2 * SUB), 2 * SUB)
                    span = slice(b * SUB, (b + 1) * SUB)
                    value = jnp.concatenate([codes[0][span], codes[1][span]], axis=0)
                    upper = value.astype(bf16)
                    factors_ref[rows, :rank] = upper
                    factors_ref[rows, rank:] = (value - upper.astype(f32)).astype(bf16)
        return carry

    lax.fori_loop(0, sources, decode, 0, unroll=4)
    total = jnp.zeros((2 * out_ref.shape[1], 2 * rank), f32)
    for g in range(factors_ref.shape[0] // group):
        factors = factors_ref[g * group : (g + 1) * group, :]
        total = total + combine(columns(right_ref, g * GROUP, GROUP, out_ref.shape[1]), factors)
    mine = factors_ref[pl.ds(pl.multiple_of(place_ref[1] * shard, shard), shard), :]
    items_ref[...] = mine[:, :rank].astype(f32) + mine[:, rank:].astype(f32)
    residual = join(total)
    found = iterate(ones_ref, factors_ref, residual, jnp.zeros_like(residual))
    for d in range(out_ref.shape[0]):
        out_ref[d] = found


def solve_held(place, ones, right, own, other, rows, copies):
    sources, chips, depth, rank = own.shape
    whole = 2 * sources * chips * (depth - SUB)
    shard = whole // sources
    return pl.pallas_call(
        held_kernel,
        out_shape=(jax.ShapeDtypeStruct((copies, rows, rank), f32), jax.ShapeDtypeStruct((shard, rank), f32)),
        in_specs=[pl.BlockSpec(memory_space=pltpu.SMEM), vspec(), vspec(), vspec(), vspec()],
        out_specs=(vspec(), vspec()),
        scratch_shapes=[pltpu.VMEM((whole, 2 * rank), bf16)],
        compiler_params=params(),
        name="solve_held",
    )(place, ones, right, own, other)


def shards(
    user_factors,
    item_factors,
    tile_user,
    tile_item,
    tile_count,
    tile_conf,
    held_user,
    held_item,
    held_count,
    held_conf,
):
    rank = user_factors.shape[1]
    chips = lax.axis_size("z")
    core = lax.axis_index("c")
    chip = lax.axis_index("z")
    me = lax.axis_index(USER)
    column = lax.axis_index(ITEM)
    peers, item_peers = lax.axis_size(USER), lax.axis_size(ITEM)
    slots = tile_user.shape[-1]
    held_slots = held_user.shape[-1]
    user_blocks = user_factors.shape[0] // BL
    item_blocks = item_factors.shape[0] // BL
    held_blocks = 2
    siblings = [(0, 1), (1, 0)]

    part = user_factors.shape[0] // item_peers
    piece, exponent = pack_users(user_factors, column, chips, part)
    piece = lax.all_to_all(piece, "z", 0, 0, tiled=True)

    blocks = peers * user_blocks * item_blocks
    order = [c * chips + z for z in range(chips) for c in range(2)]
    strips = cut_strips(
        me, tile_user[0, 0].T, tile_item[0, 0].T, tile_count[0, 0], tile_conf, exponent,
        True, order, (peers, 1), item_blocks, blocks, "cut_items",
    )
    held_all = item_peers * item_blocks * held_blocks
    held_strips = cut_strips(
        column, held_item[0, 0].T, held_user[0, 0].T, held_count[0, 0], held_conf, jnp.zeros_like(exponent),
        False, list(range(item_peers)), (1, item_blocks), held_blocks, held_all, "cut_held",
    )
    strips, held_strips, piece = lax.optimization_barrier((strips, held_strips, piece))
    strips = lax.all_to_all(strips, USER, 0, 0, tiled=True)
    own_users = lax.all_gather(piece, ITEM, axis=0, tiled=False)
    strips, own_users, held_strips = lax.optimization_barrier((strips, own_users, held_strips))
    other_users = lax.ppermute(own_users, "c", siblings)
    held_strips = lax.all_to_all(held_strips, ITEM, 0, 0, tiled=True)

    start = lax.dynamic_slice_in_dim(
        item_factors.reshape(item_blocks, peers, SUB, rank), core * chips + chip, 1, axis=1
    ).reshape(item_blocks * SUB, rank)
    mine = solve_items(start, strips, peers * slots, core.reshape(1), own_users, other_users, chips)
    mine, held_strips = lax.optimization_barrier((mine, held_strips))
    held_ones, held_right, _ = dense(held_strips, held_all, item_peers * held_slots, "dense_held")

    mine = lax.all_to_all(mine, "z", 0, 0, tiled=True)
    own = lax.all_gather(mine, ITEM, axis=0, tiled=False)
    other = lax.ppermute(own, "c", siblings)
    folded, new_items = solve_held(
        jnp.stack([core, column]), held_ones, held_right, own, other, held_blocks * SUB, item_peers
    )
    folded = lax.all_to_all(folded, ITEM, 0, 0, tiled=True)
    folded = folded.reshape(item_peers, held_blocks, SUB, rank).transpose(1, 0, 2, 3).reshape(-1, rank)
    return new_items, folded


def solution(mesh):
    split = jax.sharding.Mesh(mesh.devices.reshape(mesh.shape["user"] // 2, 2, -1, 4), ("z", "c", "y", "x"))
    in_specs = (
        P(USER, None),
        P(ITEM, None),
        P(ITEM, USER, None, None),
        P(ITEM, USER, None, None),
        P(ITEM, USER, None),
        P(ITEM, USER, None, None, None, None),
        P(USER, ITEM, None, None),
        P(USER, ITEM, None, None),
        P(USER, ITEM, None),
        P(USER, ITEM, None, None, None, None),
    )
    out_specs = (P(ITEM, None), P(USER, None))
    return jax.shard_map(shards, mesh=split, in_specs=in_specs, out_specs=out_specs, check_vma=False)
```

```python
import functools

import jax
import jax.numpy as jnp
from jax import lax
from jax.experimental import pallas as pl
from jax.experimental.pallas import tpu as pltpu
from jax.sharding import PartitionSpec as P

ITERS = 2
LAM = 1.0
EPS = 1e-6
BL = 128
SUB = 8
GROUP = 32
USER = ("z", "c")
ITEM = ("y", "x")
VMEM = 28 * 1024 * 1024

i32 = jnp.int32
f32 = jnp.float32
bf16 = jnp.bfloat16


def params():
    return pltpu.CompilerParams(vmem_limit_bytes=VMEM)


def vspec():
    return pl.BlockSpec(memory_space=pltpu.VMEM)


def power_of_two(exponent):
    bits = exponent + 126
    value = jnp.full(exponent.shape, 2.0**-126, f32)
    for k, power in enumerate((1, 2, 4, 8, 16, 32, 64)):
        value = value * jnp.where((bits >> k) & 1 == 1, f32(2.0**power), f32(1.0))
    high = jnp.where(bits >= 128, f32(2.0**64), f32(1.0))
    return value * high * high


def column_exponents(peak):
    rest = jnp.clip(peak, 2.0**-45, 2.0**60) * f32(2.0**60)
    found = jnp.zeros(peak.shape, i32)
    for k in (64, 32, 16, 8, 4, 2, 1):
        big = rest >= f32(2.0**k)
        rest = jnp.where(big, rest * f32(2.0**-k), rest)
        found = found + jnp.where(big, k, 0)
    return found - 74


def fixed_point(rows, inverse_step):
    return jnp.clip(jnp.round(rows * inverse_step), -32767.0, 32767.0).astype(i32)


def pack_users_kernel(place_ref, rows_ref, out_ref, exponent_ref):
    exponent = column_exponents(jnp.max(jnp.abs(rows_ref[...]), axis=0, keepdims=True))
    peers, part, rank = out_ref.shape
    first = pl.multiple_of(place_ref[0] * part, part)
    codes = fixed_point(rows_ref[pl.ds(first, part), :], power_of_two(-exponent)).astype(jnp.int16)
    for z in range(peers):
        out_ref[z] = codes
    exponent_ref[...] = exponent.astype(f32)


def pack_users(rows, place, peers, part):
    rank = rows.shape[1]
    return pl.pallas_call(
        pack_users_kernel,
        out_shape=(jax.ShapeDtypeStruct((peers, part, rank), jnp.int16), jax.ShapeDtypeStruct((1, rank), f32)),
        in_specs=[pl.BlockSpec(memory_space=pltpu.SMEM), vspec()],
        out_specs=(vspec(), vspec()),
        name="pack_users",
    )(place.reshape(1), rows)


def strips_kernel(turn, order, owner_scale, slot_scale, dead, place_ref, outer_ref, inner_ref, count_ref, tiles_ref, extra_ref, out_ref):
    slots, owners = outer_ref.shape
    total = owners * slots
    for t in range(0, total, 2):
        pair = [tiles_ref[t + k].astype(f32) for k in range(2)]
        if turn:
            pair = [tile.T for tile in pair]
        for d in range(len(order)):
            q = order[d] * SUB
            both = jnp.concatenate([pair[0][q : q + SUB], pair[1][q : q + SUB]], axis=0)
            out_ref[d, t * SUB : (t + 2) * SUB, :] = both.astype(bf16)
    outer_scale, owner_scale = owner_scale
    per = BL // total
    row = lax.broadcasted_iota(i32, (16, BL), 0)
    lane = lax.broadcasted_iota(i32, (16, BL), 1)
    place = place_ref[0]
    mine = jnp.where(row == place // per, lane - lax.rem(place, per) * total, -1)
    codes = jnp.zeros((16, BL), f32)
    for o in range(owners):
        for c in range(slots):
            code = (outer_ref[c, o] * outer_scale + o * owner_scale) * slot_scale + inner_ref[c, o]
            code = jnp.where(c < count_ref[o], code, dead)
            codes = jnp.where(mine == o * slots + c, code.astype(f32), codes)
    below = owners * total // BL
    for k in range(extra_ref.shape[1] // BL):
        codes = jnp.where(row == below + k, extra_ref[:, k * BL : (k + 1) * BL], codes)
    codes = codes.astype(bf16)
    for d in range(len(order)):
        out_ref[d, total * SUB :, :] = codes


def cut_strips(place, outer, inner, count, tiles, extra, turn, order, owner_scale, slot_scale, dead, name):
    slots, owners = outer.shape
    smem = pl.BlockSpec(memory_space=pltpu.SMEM)
    return pl.pallas_call(
        functools.partial(strips_kernel, turn, order, owner_scale, slot_scale, dead),
        out_shape=jax.ShapeDtypeStruct((len(order), owners * slots * SUB + 16, BL), bf16),
        in_specs=[smem, smem, smem, smem, vspec(), vspec()],
        out_specs=vspec(),
        compiler_params=params(),
        cost_estimate=pl.CostEstimate(flops=10**6, bytes_accessed=2 * 10**6, transcendentals=0),
        name=name,
    )(place.reshape(1), outer, inner, count, tiles.reshape(-1, BL, BL), extra)


def dense_kernel(blocks, slots, strips_ref, ones_ref, right_ref, step_ref, wide_ref):
    sources, depth, _ = strips_ref.shape
    count = slots * SUB
    table = strips_ref[0, count:depth, :].astype(f32)
    for s in range(1, sources):
        table = table + strips_ref[s, count:depth, :].astype(f32)
    held = sources * slots // BL
    codes = jnp.concatenate([table[k : k + 1, :] for k in range(held)], axis=1).astype(i32)
    rows = [strips_ref[s, count:depth, :].astype(f32) for s in range(sources)]
    rows = [jnp.concatenate([row[held : held + 1], row[held + 1 : held + 2]], axis=1) for row in rows]
    step_ref[...] = power_of_two(jnp.concatenate(rows, axis=0).astype(i32))
    named = lax.broadcasted_iota(i32, (blocks, sources * slots), 0) == codes
    named = jnp.where(named, f32(1.0), f32(0.0))
    live = jnp.sum(named, axis=1, keepdims=True)
    named = named.astype(bf16)
    for s in range(sources):
        wide_ref[s * count : (s + 1) * count, :] = strips_ref[s, :count, :].astype(f32)
    for r in range(0, SUB, 2):
        rows = [wide_ref[pl.ds(r + k, sources * slots, stride=SUB), :].astype(bf16) for k in range(2)]
        both = jnp.dot(named, jnp.concatenate(rows, axis=1), preferred_element_type=f32)
        for k in range(2):
            total = both[:, k * BL : (k + 1) * BL]
            ones_ref[pl.ds(r + k, blocks, stride=SUB), :] = total + 1.0
            right_ref[pl.ds(r + k, blocks, stride=SUB), :] = total + live


def dense(strips, blocks, slots, name):
    shape = jax.ShapeDtypeStruct((blocks * SUB, BL), f32)
    return pl.pallas_call(
        functools.partial(dense_kernel, blocks, slots),
        out_shape=(shape, shape, jax.ShapeDtypeStruct((strips.shape[0], 2 * BL), f32)),
        in_specs=[vspec()],
        out_specs=(vspec(), vspec(), vspec()),
        scratch_shapes=[pltpu.VMEM((strips.shape[0] * slots * SUB, BL), f32)],
        compiler_params=params(),
        cost_estimate=pl.CostEstimate(flops=4 * 10**8, bytes_accessed=3 * 10**6, transcendentals=0),
        name=name,
    )(strips)


NT = (((1,), (1,)), ((), ()))
NN = (((1,), (0,)), ((), ()))


def two_planes(value):
    upper = value.astype(bf16)
    return jnp.concatenate([upper, (value - upper.astype(f32)).astype(bf16)], axis=0)


def fold(both):
    rows = both.shape[0] // 2
    return both[:rows] + both[rows:]


def twice(planes):
    return jnp.concatenate([planes, planes], axis=1)


def scores(planes, factors):
    return fold(lax.dot_general(planes, factors, NT, preferred_element_type=f32))


def combine(weighted, factors):
    return jnp.dot(two_planes(weighted), factors, preferred_element_type=f32)


def join(both):
    rank = both.shape[1] // 2
    return fold(both[:, :rank] + both[:, rank:])


def columns(ref, first, count, rows):
    spans = [pl.ds(pl.multiple_of((first + k) * rows, rows), rows) for k in range(count)]
    return jnp.concatenate([ref[span, :] for span in spans], axis=1)


def split(codes, step):
    value = codes.astype(f32) * step
    upper = value.astype(bf16)
    return upper, (value - upper.astype(f32)).astype(bf16)


def iterate(ones_ref, factors_ref, residual, start):
    rows, rank = residual.shape
    group = GROUP * BL
    steps = factors_ref.shape[0] // group

    def operator(direction):
        planes = twice(two_planes(direction))

        def step(g, total):
            factors = factors_ref[pl.ds(pl.multiple_of(g * group, group), group), :]
            weighted = columns(ones_ref, g * GROUP, GROUP, rows) * scores(planes, factors)
            return total + combine(weighted, factors)

        total = lax.fori_loop(0, steps, step, jnp.zeros((2 * rows, 2 * rank), f32), unroll=True)
        return join(total) + LAM * direction

    def energy(direction):
        score = scores(twice(two_planes(direction)), factors_ref[...])
        weighted = columns(ones_ref, 0, factors_ref.shape[0] // BL, rows) * score
        return jnp.sum(score * weighted, axis=-1, keepdims=True) + LAM * jnp.sum(
            direction * direction, axis=-1, keepdims=True
        )

    solution = start
    direction = residual
    norm_now = jnp.sum(residual * residual, axis=-1, keepdims=True)
    for iteration in range(ITERS):
        if iteration + 1 == ITERS:
            return solution + norm_now / (energy(direction) + EPS) * direction
        image = operator(direction)
        alpha = norm_now / (jnp.sum(direction * image, axis=-1, keepdims=True) + EPS)
        solution = solution + alpha * direction
        residual = residual - alpha * image
        norm_next = jnp.sum(residual * residual, axis=-1, keepdims=True)
        direction = residual + norm_next / (norm_now + EPS) * direction
        norm_now = norm_next


def item_kernel(
    slots, start_ref, strips_ref, core_ref, own_ref, other_ref, out_ref,
    factors_ref, total_ref, ones_ref, right_ref, step_ref, wide_ref,
):
    g = pl.program_id(0)
    held = start_ref.shape[0]
    sources, chips, part, rank = own_ref.shape
    per = BL // part
    group = sources * 2 * chips * part
    core = core_ref[0]

    @pl.when(g == 0)
    def _():
        total_ref[...] = jnp.zeros_like(total_ref)
        dense_kernel(ones_ref.shape[0] // SUB, slots, strips_ref, ones_ref, right_ref, step_ref, wide_ref)

    for ref, which in ((own_ref, core), (other_ref, 1 - core)):
        for z in range(chips):
            step = step_ref[pl.ds(2 * z + which, 1), :]
            for k in range(sources):
                codes = ref[k, z].astype(i32)
                start = g * group + (k // per * 2 * chips + 2 * z + which) * BL + k % per * part
                rows = pl.ds(pl.multiple_of(start, part), part)
                factors_ref[rows, :rank], factors_ref[rows, rank:] = split(codes, step)
    factors = factors_ref[pl.ds(pl.multiple_of(g * group, group), group), :]
    count = group // BL
    score = scores(twice(two_planes(start_ref[...])), factors)
    weighted = columns(right_ref, g * count, count, held) - columns(ones_ref, g * count, count, held) * score
    total_ref[...] += combine(weighted, factors)

    @pl.when(g == pl.num_programs(0) - 1)
    def _():
        start = start_ref[...]
        found = iterate(ones_ref, factors_ref, join(total_ref[...]) - LAM * start, start)
        exponent = column_exponents(jnp.max(jnp.abs(found), axis=0, keepdims=True))
        codes = fixed_point(found, power_of_two(-exponent)).astype(jnp.int16)
        exponents = jnp.broadcast_to(exponent, (16, rank)).astype(jnp.int16)[:SUB]
        for d in range(out_ref.shape[0]):
            out_ref[d, : found.shape[0], :] = codes
            out_ref[d, found.shape[0] :, :] = exponents


def gathered_spec(shape, grid):
    return pl.BlockSpec((shape[0] // grid,) + shape[1:], lambda s: (s, 0, 0, 0))


def solve_items(start, strips, slots, core, own, other, copies):
    rows, rank = start.shape
    whole = 2 * own.size // rank
    grid = whole // (GROUP * BL)
    dense_shape = (whole // BL * rows, BL)
    codes = gathered_spec(own.shape, grid)
    return pl.pallas_call(
        functools.partial(item_kernel, slots),
        grid=(grid,),
        out_shape=jax.ShapeDtypeStruct((copies, rows + SUB, rank), jnp.int16),
        in_specs=[
            pl.BlockSpec((rows, rank), lambda s: (0, 0)),
            pl.BlockSpec(strips.shape, lambda s: (0, 0, 0), pipeline_mode=pl.Buffered(1)),
            pl.BlockSpec(memory_space=pltpu.SMEM),
            codes,
            codes,
        ],
        out_specs=pl.BlockSpec((copies, rows + SUB, rank), lambda s: (0, 0, 0)),
        scratch_shapes=[
            pltpu.VMEM((whole, 2 * rank), bf16),
            pltpu.VMEM((2 * rows, 2 * rank), f32),
            pltpu.VMEM(dense_shape, f32),
            pltpu.VMEM(dense_shape, f32),
            pltpu.VMEM((strips.shape[0], 2 * BL), f32),
            pltpu.VMEM((strips.shape[0] * slots * SUB, BL), f32),
        ],
        compiler_params=params(),
        cost_estimate=pl.CostEstimate(flops=12 * 10**9, bytes_accessed=10**7, transcendentals=0),
        name="solve_items",
    )(start, strips, core, own, other)


def held_kernel(place_ref, ones_ref, right_ref, own_ref, other_ref, out_ref, items_ref, factors_ref):
    sources, chips, depth, rank = own_ref.shape
    part = depth - SUB
    blocks = part // SUB
    shard = blocks * BL
    group = GROUP * BL
    core = place_ref[0]

    def decode(o, carry):
        for ref, which in ((own_ref, core), (other_ref, 1 - core)):
            exponents = [ref[o, z, part:depth, :].astype(i32)[:1] for z in range(chips)]
            step = power_of_two(jnp.concatenate(exponents, axis=0))
            for z in range(0, chips, 2):
                codes = [ref[o, n, :part, :].astype(i32).astype(f32) * step[n : n + 1] for n in (z, z + 1)]
                for b in range(blocks):
                    start = o * shard + b * BL + which * (BL // 2) + z * SUB
                    rows = pl.ds(pl.multiple_of(start, 2 * SUB), 2 * SUB)
                    span = slice(b * SUB, (b + 1) * SUB)
                    value = jnp.concatenate([codes[0][span], codes[1][span]], axis=0)
                    upper = value.astype(bf16)
                    factors_ref[rows, :rank] = upper
                    factors_ref[rows, rank:] = (value - upper.astype(f32)).astype(bf16)
        return carry

    lax.fori_loop(0, sources, decode, 0, unroll=8)
    total = jnp.zeros((2 * out_ref.shape[1], 2 * rank), f32)
    for g in range(factors_ref.shape[0] // group):
        factors = factors_ref[g * group : (g + 1) * group, :]
        total = total + combine(columns(right_ref, g * GROUP, GROUP, out_ref.shape[1]), factors)
    mine = factors_ref[pl.ds(pl.multiple_of(place_ref[1] * shard, shard), shard), :]
    items_ref[...] = mine[:, :rank].astype(f32) + mine[:, rank:].astype(f32)
    residual = join(total)
    found = iterate(ones_ref, factors_ref, residual, jnp.zeros_like(residual))
    for d in range(out_ref.shape[0]):
        out_ref[d] = found


def solve_held(place, ones, right, own, other, rows, copies):
    sources, chips, depth, rank = own.shape
    whole = 2 * sources * chips * (depth - SUB)
    shard = whole // sources
    return pl.pallas_call(
        held_kernel,
        out_shape=(jax.ShapeDtypeStruct((copies, rows, rank), f32), jax.ShapeDtypeStruct((shard, rank), f32)),
        in_specs=[pl.BlockSpec(memory_space=pltpu.SMEM), vspec(), vspec(), vspec(), vspec()],
        out_specs=(vspec(), vspec()),
        scratch_shapes=[pltpu.VMEM((whole, 2 * rank), bf16)],
        compiler_params=params(),
        name="solve_held",
    )(place, ones, right, own, other)


def shards(
    user_factors,
    item_factors,
    tile_user,
    tile_item,
    tile_count,
    tile_conf,
    held_user,
    held_item,
    held_count,
    held_conf,
):
    rank = user_factors.shape[1]
    chips = lax.axis_size("z")
    core = lax.axis_index("c")
    chip = lax.axis_index("z")
    me = lax.axis_index(USER)
    column = lax.axis_index(ITEM)
    peers, item_peers = lax.axis_size(USER), lax.axis_size(ITEM)
    slots = tile_user.shape[-1]
    held_slots = held_user.shape[-1]
    user_blocks = user_factors.shape[0] // BL
    item_blocks = item_factors.shape[0] // BL
    held_blocks = 2
    siblings = [(0, 1), (1, 0)]

    part = user_factors.shape[0] // item_peers
    piece, exponent = pack_users(user_factors, column, chips, part)
    piece = lax.all_to_all(piece, "z", 0, 0, tiled=True)

    blocks = peers * user_blocks * item_blocks
    order = [c * chips + z for z in range(chips) for c in range(2)]
    strips = cut_strips(
        me, tile_user[0, 0].T, tile_item[0, 0].T, tile_count[0, 0], tile_conf, exponent,
        True, order, (peers, 1), item_blocks, blocks, "cut_items",
    )
    held_all = item_peers * item_blocks * held_blocks
    held_strips = cut_strips(
        column, held_item[0, 0].T, held_user[0, 0].T, held_count[0, 0], held_conf, jnp.zeros_like(exponent),
        False, list(range(item_peers)), (1, item_blocks), held_blocks, held_all, "cut_held",
    )
    strips, held_strips, piece = lax.optimization_barrier((strips, held_strips, piece))
    strips = lax.all_to_all(strips, USER, 0, 0, tiled=True)
    own_users = lax.all_gather(piece, ITEM, axis=0, tiled=False)
    strips, own_users, held_strips = lax.optimization_barrier((strips, own_users, held_strips))
    other_users = lax.ppermute(own_users, "c", siblings)
    held_strips = lax.all_to_all(held_strips, ITEM, 0, 0, tiled=True)

    start = lax.dynamic_slice_in_dim(
        item_factors.reshape(item_blocks, peers, SUB, rank), core * chips + chip, 1, axis=1
    ).reshape(item_blocks * SUB, rank)
    mine = solve_items(start, strips, peers * slots, core.reshape(1), own_users, other_users, chips)
    mine, held_strips = lax.optimization_barrier((mine, held_strips))
    held_ones, held_right, _ = dense(held_strips, held_all, item_peers * held_slots, "dense_held")

    mine = lax.all_to_all(mine, "z", 0, 0, tiled=True)
    own = lax.all_gather(mine, ITEM, axis=0, tiled=False)
    other = lax.ppermute(own, "c", siblings)
    folded, new_items = solve_held(
        jnp.stack([core, column]), held_ones, held_right, own, other, held_blocks * SUB, item_peers
    )
    folded = lax.all_to_all(folded, ITEM, 0, 0, tiled=True)
    folded = folded.reshape(item_peers, held_blocks, SUB, rank).transpose(1, 0, 2, 3).reshape(-1, rank)
    return new_items, folded


def solution(mesh):
    split = jax.sharding.Mesh(mesh.devices.reshape(mesh.shape["user"] // 2, 2, -1, 4), ("z", "c", "y", "x"))
    in_specs = (
        P(USER, None),
        P(ITEM, None),
        P(ITEM, USER, None, None),
        P(ITEM, USER, None, None),
        P(ITEM, USER, None),
        P(ITEM, USER, None, None, None, None),
        P(USER, ITEM, None, None),
        P(USER, ITEM, None, None),
        P(USER, ITEM, None),
        P(USER, ITEM, None, None, None, None),
    )
    out_specs = (P(ITEM, None), P(USER, None))
    return jax.shard_map(shards, mesh=split, in_specs=in_specs, out_specs=out_specs, check_vma=False)
```
